32 devices in a mesh: groups: 2 (over x), rows: 8 (over z, y), cols: 2 (over core).
Axes of the slice: x: 2, y: 2, z: 4, core: 2. Of those that a mesh axis runs over, the one named last changes fastest.
Arguments:
- radiosity: bfloat16 [4, 98304], P(None, ('groups', 'rows', 'cols')), parts along dimension 1, may hold values from 0.099609375 to 4
- emission: float32 [4, 98304], P(None, ('groups', 'rows', 'cols')), parts along dimension 1, may hold values from 0.05 to 2
- material: int32 [98304], P(('groups', 'rows', 'cols')), parts along dimension 0, may hold values from 0 to 15
- reflectance: float32 [4, 16], replicated, may hold values from 0.1 to 0.9
- static_tiles: bfloat16 [16, 2, 64, 128, 128], P(('groups', 'rows'), 'cols'), parts along dimension 0, may hold values from 0.00019931793 to 0.0079956055
- static_index: int32 [16, 2, 2, 64], P(('groups', 'rows'), 'cols'), parts along dimension 0, may hold values from 0 to 191, as said below
- row_geometry: float32 [6, 4, 98304], P(None, None, ('groups', 'rows')), parts along dimension 2, as said below
- array_geometry: float32 [4, 8, 6, 4, 4096], P(('groups', 'cols'), 'rows'), parts along dimension 0, as said below
- array_owner: int32 [4], P(('groups', 'cols')), parts along dimension 0, may hold values from 0 to 7
- array_index: int32 [16, 2, 2, 16], P(('groups', 'rows')), parts along dimension 0, may hold values from 0 to 47, as said below
- array_count: int32 [16, 2], P(('groups', 'rows')), parts along dimension 0, may hold values from 1 to 16, as said below
- visibility: int32 [16, 2, 16, 128, 128], P(('groups', 'rows'), 'cols'), parts along dimension 0, may hold values 0 or 1
Outputs:
- new_radiosity: float32 [4, 98304], P(None, ('groups', 'rows', 'cols')), parts along dimension 1
The draws below stay inside these ranges and needn't reach their ends.
There are 2 independent parts, one for each index of `groups`. The reference program is written for one: setup_inputs(seed, part) draws one part's arguments, and reference() takes and returns one part's arrays. A program takes and returns all parts, laid end to end along the dimension named above; an argument that names none is the same for every part. Nothing has to cross between parts.
Inputs may be any that keep to these rules, and one draw needn't show every extreme that they name: `static_index`: within one entry [r, g] the 64 pairs (row tile, column tile) are distinct, row tiles below 48. `array_index`: within one entry [r, g] the 16 pairs (row tile, array tile) are distinct, row tiles below 48, array tiles below 32; slots at or after the count are not used. `array_count`: some entry equals 16 in every draw. `row_geometry`: positions in a box of side 2, areas between 0.005 and 0.05. `array_geometry`: positions in a box of side 2, areas between 0.005 and 0.05.
All inputs are finite; a program needn't handle non-finite values. No bound on the sum of `visibility` on one device may be relied on, other than what follows from the above.
Results may differ from the reference program's by a relative error of at most 0.0003.
Values may be sent and summed in bfloat16 or wider, within the bound.
No kernel may reach another device: no remote copies, remote signals or barrier semaphores. Data moves between devices by JAX's collectives and lax.ppermute only.
A program may use at most 64 MiB of HBM per device.

```python
import math
import jax
import jax.numpy as jnp
from jax import lax

TILE = 128
POINTS = 4
BANDS = 4
MATERIALS = 16
ARRAY_PATCHES = 4096
ROW_TILES = 48
STORED = 64
SLOTS = 16
PATCHES = 49152
PATCH_DEV = 3072
COL_TILES = 192
ARRAY_TILES = 32
N_ROWS = 8
N_COLS = 2


def draw_fields(key, leading, length):
    first_key, second_key, third_key = jax.random.split(key, 3)
    places = jax.random.uniform(first_key, leading + (3, POINTS, length), jnp.float32, -1.0, 1.0)
    angles = jax.random.uniform(second_key, leading + (2, POINTS, length), jnp.float32, -math.pi, math.pi)
    areas = jnp.exp(jax.random.uniform(third_key, leading + (1, POINTS, length), jnp.float32, math.log(0.005), math.log(0.05)))
    return jnp.concatenate([places, angles, areas], axis=len(leading))


def draw_row_geometry(key, part):
    return draw_fields(jax.random.fold_in(key, 11), (), PATCHES)


def draw_array_geometry(key, part):
    return draw_fields(jax.random.fold_in(key, 12), (N_COLS, N_ROWS), ARRAY_PATCHES)


def distinct_pairs(key, second_count, taken):
    subkeys = jax.random.split(key, N_ROWS * N_COLS)
    shuffled = jax.vmap(lambda sub: jax.random.permutation(sub, ROW_TILES * second_count)[:taken])(subkeys)
    shuffled = shuffled.astype(jnp.int32)
    paired = jnp.stack([shuffled // second_count, shuffled % second_count], axis=1)
    return paired.reshape(N_ROWS, N_COLS, 2, taken).astype(jnp.int32)


def draw_static_index(key, part):
    return distinct_pairs(jax.random.fold_in(key, 13), COL_TILES, STORED)


def draw_array_index(key, part):
    return distinct_pairs(jax.random.fold_in(key, 14), ARRAY_TILES, SLOTS)


def draw_array_count(key, part):
    first_key, second_key, third_key = jax.random.split(jax.random.fold_in(key, 15), 3)
    device_total = N_ROWS * N_COLS
    loaded = jax.random.randint(first_key, (device_total,), 0, 8) == 0
    forced = jax.random.randint(second_key, (), 0, device_total)
    loaded = jnp.logical_or(loaded, jnp.arange(device_total, dtype=jnp.int32) == forced)
    lighter = jax.random.randint(third_key, (device_total,), 1, max(2, SLOTS // 4) + 1)
    counts = jnp.where(loaded, SLOTS, lighter)
    return counts.reshape(N_ROWS, N_COLS).astype(jnp.int32)


def touch_ends(drawn, stream_key, smallest, largest):
    longest = drawn.shape.index(max(drawn.shape))
    spots = []
    for shift in (0, 1):
        where = [jax.random.randint(jax.random.fold_in(stream_key, axis), (), 0, length) for axis, length in enumerate(drawn.shape)]
        where[longest] = (where[longest] + shift) % drawn.shape[longest]
        spots.append(tuple(where))
    return drawn.at[spots[0]].set(smallest).at[spots[1]].set(largest)


def levels(stream_key, shape, cuts, least, top_value):
    factor_of, own = 1.0, jax.random.fold_in(stream_key, 6)
    for position, blocks in cuts:
        heights = jnp.exp(jax.random.uniform(jax.random.fold_in(own, position), (blocks,), jnp.float32, least / len(cuts), top_value / len(cuts)))
        factor_of = factor_of * jnp.repeat(heights, shape[position] // blocks).reshape([-1 if axis == position else 1 for axis in range(len(shape))])
    return factor_of


def setup_inputs(seed: int = 0, part: int = 0) -> dict:
    seeds = jax.random.split(jax.random.key(seed), 13)
    part_keys = jax.random.split(jax.random.fold_in(seeds[12], part), 13)
    return {
        "radiosity": jnp.clip(jnp.exp(math.log(4.0) - 3.6927934 * jax.random.uniform(part_keys[0], (BANDS, PATCHES), jnp.float32) ** levels(part_keys[0], (BANDS, PATCHES), ((1, 16),), -0.2, 0.2)), 0.099609375, 4.0).astype(jnp.bfloat16),
        "emission": jnp.clip(jnp.exp(math.log(2.0) - 3.6888794 * jax.random.uniform(part_keys[1], (BANDS, PATCHES), jnp.float32) ** levels(part_keys[1], (BANDS, PATCHES), ((1, 16),), -0.2, 0.2)), 0.05, 2.0),
        "material": touch_ends(jax.random.randint(part_keys[2], (PATCHES,), 0, MATERIALS), jax.random.fold_in(part_keys[2], 1), 0, MATERIALS - 1).astype(jnp.int32),
        "reflectance": jnp.clip(jax.random.uniform(seeds[3], (BANDS, MATERIALS), jnp.float32, 0.1, 0.9), 0.1, 0.9),
        "static_tiles": jnp.clip(jnp.exp(math.log(0.0079956055) - 3.6917462 * jax.random.uniform(part_keys[4], (N_ROWS, N_COLS, STORED, TILE, TILE), jnp.float32) ** levels(part_keys[4], (N_ROWS, N_COLS, STORED, TILE, TILE), ((0, 8), (1, 2)), -0.2, 0.2)), 0.00019931793, 0.0079956055).astype(jnp.bfloat16),
        "static_index": draw_static_index(jax.random.fold_in(jax.random.fold_in(seeds[12], part), 71), part),
        "row_geometry": draw_row_geometry(jax.random.fold_in(jax.random.fold_in(seeds[12], part), 71), part),
        "array_geometry": draw_array_geometry(jax.random.fold_in(jax.random.fold_in(seeds[12], part), 71), part),
        "array_owner": jax.random.randint(part_keys[8], (N_COLS,), 0, N_ROWS).astype(jnp.int32),
        "array_index": draw_array_index(jax.random.fold_in(jax.random.fold_in(seeds[12], part), 71), part),
        "array_count": draw_array_count(jax.random.fold_in(jax.random.fold_in(seeds[12], part), 71), part),
        "visibility": touch_ends((jax.random.randint(part_keys[11], (N_ROWS, N_COLS, SLOTS, TILE, TILE), 0, 4) < 3).astype(jnp.int32), jax.random.fold_in(part_keys[11], 1), 0, 1),
    }


def unit_normal(polar_angle, azimuth):
    return jnp.stack([jnp.sin(polar_angle) * jnp.cos(azimuth), jnp.sin(polar_angle) * jnp.sin(azimuth), jnp.cos(polar_angle)])


def kernel_tile(row_points, col_points):
    offset = col_points[0:3][:, None, None, :, :] - row_points[0:3][:, :, :, None, None]
    row_normal = unit_normal(row_points[3], row_points[4])
    col_normal = unit_normal(col_points[3], col_points[4])
    facing = jnp.sum(row_normal[:, :, :, None, None] * offset, axis=0)
    toward = jnp.sum(col_normal[:, None, None, :, :] * offset, axis=0)
    spread = jnp.sum(offset * offset, axis=0)
    col_area = col_points[5][None, None, :, :]
    kernel_value = jnp.maximum(facing, 0.0) * jnp.maximum(-toward, 0.0) * col_area / (math.pi * (spread + col_area) ** 2)
    return jnp.sum(kernel_value, axis=(0, 2)) / POINTS


def tile_rows(products, row_ids):
    onehot = (row_ids[:, None] == jnp.arange(ROW_TILES, dtype=jnp.int32)[None, :]).astype(jnp.float32)
    return jnp.einsum("kbp,kr->brp", products, onehot, precision=lax.Precision.HIGHEST)


def reference(radiosity, emission, material, reflectance, static_tiles, static_index, row_geometry, array_geometry, array_owner, array_index, array_count, visibility):
    row_length = ROW_TILES * TILE
    gathered = radiosity.reshape(BANDS, N_ROWS, N_COLS, PATCH_DEV).transpose(0, 2, 1, 3).reshape(BANDS, N_COLS, COL_TILES, TILE).astype(jnp.float32)
    first_array = COL_TILES - ARRAY_TILES

    def one_block(row_block):
        summed = jnp.zeros((BANDS, ROW_TILES, TILE), jnp.float32)
        row_points = lax.dynamic_slice_in_dim(row_geometry, row_block * row_length, row_length, 2)
        for col_group in range(N_COLS):
            stored = static_tiles[row_block, col_group].astype(jnp.float32)
            positions = static_index[row_block, col_group]
            slices = jnp.take(gathered[:, col_group], positions[1], axis=1)
            products = jnp.einsum("kps,bks->kbp", stored, slices, precision=lax.Precision.HIGHEST)
            summed = summed + tile_rows(products, positions[0])
            points = array_geometry[col_group, array_owner[col_group]]
            slot_list = array_index[row_block, col_group]
            live_count = array_count[row_block, col_group]
            visible = visibility[row_block, col_group]

            def make_tile(slot_index):
                row_slab = lax.dynamic_slice_in_dim(row_points, slot_list[0, slot_index] * TILE, TILE, 2)
                array_slab = lax.dynamic_slice_in_dim(points, slot_list[1, slot_index] * TILE, TILE, 2)
                one_tile = kernel_tile(row_slab, array_slab)
                one_tile = one_tile * visible[slot_index].astype(one_tile.dtype)
                return jnp.where(slot_index < live_count, one_tile, jnp.zeros_like(one_tile))

            rebuilt = lax.map(make_tile, jnp.arange(SLOTS, dtype=jnp.int32))
            array_slices = jnp.take(gathered[:, col_group], first_array + slot_list[1], axis=1)
            products = jnp.einsum("kps,bks->kbp", rebuilt, array_slices, precision=lax.Precision.HIGHEST)
            summed = summed + tile_rows(products, slot_list[0])
        return summed.reshape(BANDS, row_length)

    blocks = lax.map(one_block, jnp.arange(N_ROWS, dtype=jnp.int32))
    rows_sum = blocks.transpose(1, 0, 2).reshape(BANDS, PATCHES)
    albedo = reflectance[:, material]
    return emission + albedo * rows_sum
```

```python
import functools
import math

import jax
import jax.numpy as jnp
from jax import lax
from jax.experimental import pallas as pl
from jax.experimental.pallas import tpu as pltpu
from jax.sharding import PartitionSpec as P

TILE = 128
POINTS = 4
POS = 2.0**14
MOM = 2.0**19
RAD = 2.0**11
REFS = 8
GROUP = 16 * 12
F32 = jnp.float32
BF16 = jnp.bfloat16
VMEM = pltpu.VMEM
NT = (((1,), (1,)), ((), ()))


def whole(memory_space=VMEM):
    return pl.BlockSpec(memory_space=memory_space)


def parts3(value):
    first = value.astype(BF16)
    rest = value - first.astype(F32)
    second = rest.astype(BF16)
    third = (rest - second.astype(F32)).astype(BF16)
    return first, second, third


def encode_kernel(half_tiles, geo_ref, rad_ref, keep_ref, send_ref, halves):
    lower = lax.axis_index("rows") & 1
    half_rows = 12 * half_tiles + REFS
    angles = jnp.concatenate([geo_ref[3], geo_ref[4]], axis=0)
    sines, cosines = jnp.sin(angles), jnp.cos(angles)
    area = geo_ref[5]
    normal = (
        sines[0:4] * cosines[4:8],
        sines[0:4] * sines[4:8],
        cosines[0:4],
    )
    for axis in range(3):
        place = geo_ref[axis]
        low = jnp.min(jnp.min(place, axis=1, keepdims=True), axis=0, keepdims=True)
        high = jnp.max(jnp.max(place, axis=1, keepdims=True), axis=0, keepdims=True)
        centre = jnp.floor((low + high) * 0.5 + 0.5)
        moved = jnp.floor((place - centre) * POS + 0.5).astype(jnp.int32)
        moved = jnp.clip(moved, -32768, 32767)
        moment = jnp.floor(area * normal[axis] * MOM + 0.5).astype(jnp.int32)
        moment = jnp.clip(moment, -32768, 32767)
        words = (moved << 16) | (moment & 65535)
        for tile in range(2 * half_tiles):
            row = 12 * (tile % half_tiles) + 4 * axis
            halves[tile // half_tiles, row : row + 4, :] = words[:, tile * TILE : (tile + 1) * TILE]
        whole_centre = jnp.broadcast_to(centre.astype(jnp.int32), (1, TILE))
        for half in range(2):
            row = half_rows - REFS + axis
            halves[half, row : row + 1, :] = whole_centre
    for half in range(2):
        halves[half, half_rows - REFS + 3 :, :] = jnp.zeros((REFS - 3, TILE), jnp.int32)
    keep_ref[...] = halves[lower]
    send_ref[0:half_rows, :] = halves[1 - lower]
    rad = (rad_ref[...].astype(F32) * RAD).astype(jnp.int32)
    rad = (rad[0:2] << 16) | rad[2:4]
    for tile in range(rad.shape[1] // TILE):
        row = half_rows + 2 * tile
        send_ref[row : row + 2, :] = rad[:, tile * TILE : (tile + 1) * TILE]


def rows_kernel(list_ref, count_ref, centre_ref, geo_ref, facing_ref, place_ref, columns):
    group = lax.axis_index("cols")
    columns[...] = jnp.zeros_like(columns)
    lane_row = lax.broadcasted_iota(jnp.int32, (8, TILE), 0)
    ones = jnp.where(lane_row < 3, 1.0, 0.0).astype(F32)
    blank = jnp.zeros((8, TILE), F32)

    def one_slot(slot, carry):
        start = pl.multiple_of(list_ref[group, 0, slot] * TILE, TILE)
        slab = [geo_ref[field, :, pl.ds(start, TILE)] for field in range(5)]
        place = [slab[axis] - centre_ref[axis : axis + 1, :] for axis in range(3)]
        sine = jnp.sin(slab[3])
        normal = (sine * jnp.cos(slab[4]), sine * jnp.sin(slab[4]), jnp.cos(slab[3]))
        shift = -(normal[0] * place[0] + normal[1] * place[1] + normal[2] * place[2])
        square = place[0] * place[0] + place[1] * place[1] + place[2] * place[2]

        def put(row, value):
            columns[pl.ds(row, POINTS, stride=64), :] = value.astype(F32)

        for axis in range(3):
            for part, value in enumerate(parts3(normal[axis])):
                put(8 * part + axis, value)
            for part, value in enumerate(parts3(place[axis])):
                put(32 + 8 * part + axis, value)
        for part, value in enumerate(parts3(shift)):
            put(24 + part, value)
        for part, value in enumerate(parts3(square)):
            put(56 + part, value)
        for point in range(POINTS):
            block = [columns[64 * point + 8 * i : 64 * point + 8 * i + 8, :] for i in range(8)]
            n1, n2, n3, c, x1, x2, x3, q = block
            facing = jnp.concatenate([n1, n1, n1, n2, n2, n3, c, blank], axis=0)
            places = jnp.concatenate([q, x1, x1, x1, x2, x2, x3, ones], axis=0)
            at = pl.ds(point * TILE, TILE)
            facing_ref[slot, at, :] = facing.T.astype(BF16)
            place_ref[slot, at, :] = places.T.astype(BF16)
        return carry

    lax.fori_loop(0, count_ref[group], one_slot, 0)


def main_kernel(
    half_tiles,
    out_tiles,
    list_ref,
    count_ref,
    static_ref,
    spot_ref,
    array_spot_ref,
    centre_ref,
    facing_ref,
    place_ref,
    visible_ref,
    rad_ref,
    own_ref,
    other_ref,
    tiles_ref,
    keep_ref,
    send_ref,
    words,
    total,
):
    group = lax.axis_index("cols")
    lower = lax.axis_index("rows") & 1
    half_rows = 12 * half_tiles + REFS
    total[...] = jnp.zeros_like(total)

    def radiosity(spot):
        pair = rad_ref[pl.ds(2 * spot, 2), :]
        both = jnp.concatenate([pair >> 16, pair & 65535], axis=0)
        return (both.astype(F32) * (1.0 / RAD)).astype(BF16)

    def one_tile(index, carry):
        part = lax.dot_general(
            radiosity(spot_ref[index]), tiles_ref[index], NT, preferred_element_type=F32
        )
        row = static_ref[0, index]
        total[row] = total[row] + part
        return carry

    lax.fori_loop(0, tiles_ref.shape[0], one_tile, 0, unroll=4)

    words[0, 0:half_rows, :] = own_ref[...]
    words[1, 0:half_rows, :] = other_ref[...]
    sub = lax.broadcasted_iota(jnp.int32, (8, POINTS * TILE), 0)
    valid = sub < 3
    away = own_ref[half_rows - REFS :, :].astype(F32) - centre_ref[...]
    away = jnp.concatenate([away] * POINTS, axis=1)
    blank = jnp.zeros((8, POINTS * TILE), F32)
    ones = jnp.where(valid, 1.0, 0.0).astype(F32)

    def stack3(value):
        first, second, third = parts3(value)
        first, second, third = first.astype(F32), second.astype(F32), third.astype(F32)
        return jnp.where(sub == 0, first, jnp.where(sub == 1, second, jnp.where(valid, third, 0.0)))

    def split(value):
        return [part.astype(F32) for part in parts3(value)]

    def one_slot(slot, carry):
        tile = list_ref[group, 1, slot]
        half = (tile // half_tiles) ^ lower
        start = (tile % half_tiles) * 12
        word = jnp.concatenate(
            [words[half, pl.ds(start + point, 8, stride=POINTS), :] for point in range(POINTS)],
            axis=1,
        )
        place = jnp.where(valid, (word >> 16).astype(F32) * (1.0 / POS) + away, 0.0)
        moment = jnp.where(valid, ((word << 16) >> 16).astype(F32) * (1.0 / MOM), 0.0)
        area = jnp.sqrt(jnp.sum(moment * moment, axis=0, keepdims=True))
        shift = stack3(-jnp.sum(moment * place, axis=0, keepdims=True))
        square = stack3(jnp.sum(place * place, axis=0, keepdims=True) + area)
        x1, x2, x3 = split(place)
        m1, m2, m3 = split(moment)
        y1, y2, y3 = -2.0 * x1, -2.0 * x2, -2.0 * x3
        right_f = jnp.concatenate([x1, x2, x3, x1, x2, x1, ones, blank], axis=0).astype(BF16)
        right_t = jnp.concatenate([blank, m1, m2, m3, m1, m2, m1, shift], axis=0).astype(BF16)
        right_s = jnp.concatenate([ones, y1, y2, y3, y1, y2, y1, square], axis=0).astype(BF16)
        gain = None
        for point in range(POINTS):
            left_f = facing_ref[slot, point * TILE : (point + 1) * TILE, :]
            left_x = place_ref[slot, point * TILE : (point + 1) * TILE, :]
            facing = jnp.dot(left_f, right_f, preferred_element_type=F32)
            toward = jnp.dot(left_x, right_t, preferred_element_type=F32)
            spread = jnp.dot(left_x, right_s, preferred_element_type=F32)
            over = jnp.maximum(facing, 0.0) * jnp.maximum(toward, 0.0)
            under = spread * spread
            for first, second in ((0, 1), (2, 3)):
                a = slice(first * TILE, (first + 1) * TILE)
                b = slice(second * TILE, (second + 1) * TILE)
                term = (over[:, a] * under[:, b] + over[:, b] * under[:, a]) / (
                    under[:, a] * under[:, b]
                )
                gain = term if gain is None else gain + term
        gain = gain * visible_ref[slot].astype(F32)
        high = gain.astype(BF16)
        low = (gain - high.astype(F32)).astype(BF16)
        rad = radiosity(array_spot_ref[slot])
        part = lax.dot_general(rad, high, NT, preferred_element_type=F32)
        part = part + lax.dot_general(rad, low, NT, preferred_element_type=F32)
        row = list_ref[group, 0, slot]
        total[row] = total[row] + part * (1.0 / (math.pi * POINTS))
        return carry

    lax.fori_loop(0, count_ref[group], one_slot, 0)
    for tile in range(out_tiles):
        at = slice(tile * TILE, (tile + 1) * TILE)
        keep_ref[:, at] = total[group * out_tiles + tile]
        send_ref[:, at] = total[(1 - group) * out_tiles + tile]


def body(
    radiosity,
    emission,
    material,
    reflectance,
    static_tiles,
    static_index,
    row_geometry,
    array_geometry,
    array_owner,
    array_index,
    array_count,
    visibility,
):
    rows = lax.axis_size("rows")
    me = lax.axis_index("rows")
    owner = array_owner[0]
    bands, patches = radiosity.shape
    own_tiles = patches // TILE
    row_tiles = row_geometry.shape[2] // TILE
    array_tiles = array_geometry.shape[-1] // TILE
    half_tiles = array_tiles // 2
    half_rows = 12 * half_tiles + REFS
    rad_rows = 2 * own_tiles
    slots = visibility.shape[2]
    column_tiles = own_tiles * rows

    spread_bits = [rows >> shift for shift in range(1, rows.bit_length() - 1)]
    order = [1] + spread_bits

    def hop(value, bit):
        return lax.ppermute(value, "rows", [(i, i ^ bit) for i in range(rows)])

    def better(mine, theirs, bit):
        return jnp.where(((owner ^ me) & bit) != 0, theirs, mine)

    keep, send = pl.pallas_call(
        functools.partial(encode_kernel, half_tiles),
        out_shape=(
            jax.ShapeDtypeStruct((half_rows, TILE), jnp.int32),
            jax.ShapeDtypeStruct((half_rows + rad_rows, TILE), jnp.int32),
        ),
        in_specs=[whole(), whole()],
        out_specs=(whole(), whole()),
        scratch_shapes=[VMEM((2, half_rows, TILE), jnp.int32)],
        name="encode",
    )(array_geometry[0, 0], radiosity)

    rad = send[half_rows:]
    for bit in order:
        got = hop(send, bit)
        keep = better(keep, got[:half_rows], bit)
        rad = jnp.concatenate([rad, got[half_rows:]], axis=0)
        send = jnp.concatenate([keep, rad], axis=0)
    other = hop(keep, 1)

    def spot(column_tile):
        holder = (column_tile // own_tiles) ^ me
        place = jnp.zeros_like(column_tile)
        for level, bit in enumerate(order):
            place = place + jnp.where((holder & bit) != 0, 1 << level, 0)
        return place * own_tiles + column_tile % own_tiles

    group = lax.axis_index("cols")
    lists = array_index[0]
    counts = array_count[0]
    static_list = static_index[0, 0]
    static_spot = spot(static_list[1])
    array_spot = spot(column_tiles - array_tiles + lists[group, 1])
    row_centre = jnp.round(row_geometry[0:3, 0, 0])
    row_centre = jnp.pad(jnp.broadcast_to(row_centre[:, None], (3, TILE)), ((0, 5), (0, 0)))

    facing, place = pl.pallas_call(
        rows_kernel,
        out_shape=(jax.ShapeDtypeStruct((slots, POINTS * TILE, 64), BF16),) * 2,
        in_specs=[whole(pltpu.SMEM), whole(pltpu.SMEM), whole(), whole()],
        out_specs=(whole(), whole()),
        scratch_shapes=[VMEM((POINTS * 64, TILE), F32)],
        name="rows",
    )(lists, counts, row_centre, row_geometry)

    onehot = (jnp.arange(reflectance.shape[1], dtype=jnp.int32)[:, None] == material[None, :]).astype(F32)
    albedo = jnp.dot(reflectance, onehot, precision=lax.Precision.HIGHEST)

    shape = jax.ShapeDtypeStruct((bands, patches), F32)
    smem = whole(pltpu.SMEM)
    kept, sent = pl.pallas_call(
        functools.partial(main_kernel, half_tiles, row_tiles // 2),
        out_shape=(shape, shape),
        in_specs=[smem] * 5 + [whole()] * 8,
        out_specs=(whole(), whole()),
        scratch_shapes=[
            VMEM((2, half_rows + 16, TILE), jnp.int32),
            VMEM((row_tiles, bands, TILE), F32),
        ],
        compiler_params=pltpu.CompilerParams(vmem_limit_bytes=40 << 20),
        name="main",
    )(
        lists,
        counts,
        static_list,
        static_spot,
        array_spot,
        row_centre,
        facing,
        place,
        visibility[0, 0],
        rad,
        keep,
        other,
        static_tiles[0, 0],
    )
    arrived = lax.ppermute(sent, "cols", [(0, 1), (1, 0)])
    return emission + albedo * (kept + arrived)


def solution(mesh):
    in_specs = (
        P(None, ("groups", "rows", "cols")),
        P(None, ("groups", "rows", "cols")),
        P(("groups", "rows", "cols")),
        P(),
        P(("groups", "rows"), "cols", None, None, None),
        P(("groups", "rows"), "cols", None, None),
        P(None, None, ("groups", "rows")),
        P(("groups", "cols"), "rows", None, None, None),
        P(("groups", "cols")),
        P(("groups", "rows"), None, None, None),
        P(("groups", "rows"), None),
        P(("groups", "rows"), "cols", None, None, None),
    )
    out_specs = P(None, ("groups", "rows", "cols"))
    return jax.shard_map(body, mesh=mesh, in_specs=in_specs, out_specs=out_specs, check_vma=False)
```

```python
import functools
import math

import jax
import jax.numpy as jnp
from jax import lax
from jax.experimental import pallas as pl
from jax.experimental.pallas import tpu as pltpu
from jax.sharding import PartitionSpec as P

TILE = 128
POINTS = 4
POS = 2.0**14
MOM = 2.0**19
RAD = 2.0**11
CHUNKS = 8
REFS = 8
GROUP = 16 * 12
F32 = jnp.float32
BF16 = jnp.bfloat16
VMEM = pltpu.VMEM
NT = (((1,), (1,)), ((), ()))


def hop_orders(rows):
    high = [rows >> shift for shift in range(1, rows.bit_length() - 1)]
    return [1] + high, high + [1]


def bit_of(level, rows):
    first, second = hop_orders(rows)
    return jnp.where(lax.axis_index("cols") == 0, first[level], second[level])


def held_half():
    return ((lax.axis_index("rows") & bit_of(0, lax.axis_size("rows"))) != 0).astype(jnp.int32)


def whole(memory_space=VMEM):
    return pl.BlockSpec(memory_space=memory_space)


def in_hbm(value):
    return pltpu.with_memory_space_constraint(value, pltpu.HBM)


def parts3(value):
    first = value.astype(BF16)
    rest = value - first.astype(F32)
    second = rest.astype(BF16)
    third = (rest - second.astype(F32)).astype(BF16)
    return first, second, third


def encode_kernel(
    half_tiles, geo_hbm, rad_hbm, keep_ref, send_ref, words_ref, geo_ref, rad_ref, arrived, halves
):
    lower = held_half()
    half_rows = 12 * half_tiles + REFS
    fields = [
        pltpu.make_async_copy(geo_hbm.at[field], geo_ref.at[field], arrived.at[field]) for field in range(6)
    ]
    for field in (3, 4, 5, 0, 1, 2):
        fields[field].start()
    own_rad = pltpu.make_async_copy(rad_hbm, rad_ref, arrived.at[6])
    own_rad.start()
    for field in (3, 4, 5):
        fields[field].wait()
    angles = jnp.concatenate([geo_ref[3], geo_ref[4]], axis=0)
    sines, cosines = jnp.sin(angles), jnp.cos(angles)
    area = geo_ref[5]
    normal = (
        sines[0:4] * cosines[4:8],
        sines[0:4] * sines[4:8],
        cosines[0:4],
    )
    for axis in range(3):
        fields[axis].wait()
        place = geo_ref[axis]
        low = jnp.min(jnp.min(place, axis=1, keepdims=True), axis=0, keepdims=True)
        high = jnp.max(jnp.max(place, axis=1, keepdims=True), axis=0, keepdims=True)
        centre = jnp.floor((low + high) * 0.5 + 0.5)
        moved = jnp.floor((place - centre) * POS + 0.5).astype(jnp.int32)
        moved = jnp.clip(moved, -32768, 32767)
        moment = jnp.floor(area * normal[axis] * MOM + 0.5).astype(jnp.int32)
        moment = jnp.clip(moment, -32768, 32767)
        words = (moved << 16) | (moment & 65535)
        for tile in range(2 * half_tiles):
            row = 12 * (tile % half_tiles) + 4 * axis
            halves[tile // half_tiles, row : row + 4, :] = words[:, tile * TILE : (tile + 1) * TILE]
        whole_centre = jnp.broadcast_to(centre.astype(jnp.int32), (1, TILE))
        for half in range(2):
            row = half_rows - REFS + axis
            halves[half, row : row + 1, :] = whole_centre
    for half in range(2):
        halves[half, half_rows - REFS + 3 :, :] = jnp.zeros((REFS - 3, TILE), jnp.int32)
    keep_ref[...] = halves[lower]
    send_ref[0:half_rows, :] = halves[1 - lower]
    own_rad.wait()
    rad = (rad_ref[...].astype(F32) * RAD).astype(jnp.int32)
    rad = (rad[0:2] << 16) | rad[2:4]
    for tile in range(rad.shape[1] // TILE):
        words_ref[2 * tile : 2 * tile + 2, :] = rad[:, tile * TILE : (tile + 1) * TILE]
    send_ref[half_rows:, :] = words_ref[...]


def rows_kernel(list_ref, count_ref, geo_hbm, left_ref, centre_ref, geo_ref, arrived, columns):
    copy = pltpu.make_async_copy(geo_hbm, geo_ref, arrived)
    copy.start()
    group = lax.axis_index("cols")
    columns[...] = jnp.zeros_like(columns)
    lane_row = lax.broadcasted_iota(jnp.int32, (8, TILE), 0)
    ones = jnp.where(lane_row < 3, 1.0, 0.0).astype(F32)
    blank = jnp.zeros((8, TILE), F32)
    centre_ref[...] = blank
    copy.wait()
    centre = []
    for axis in range(3):
        first = jnp.floor(geo_ref[axis, 0:1, 0:1] + 0.5)
        centre.append(first)
        centre_ref[axis : axis + 1, :] = jnp.broadcast_to(first, (1, TILE))

    def one_slot(slot, carry):
        start = pl.multiple_of(list_ref[group, 0, slot] * TILE, TILE)
        slab = [geo_ref[field, :, pl.ds(start, TILE)] for field in range(5)]
        place = [slab[axis] - centre[axis] for axis in range(3)]
        angles = jnp.concatenate([slab[3], slab[4]], axis=0)
        sines, cosines = jnp.sin(angles), jnp.cos(angles)
        normal = (sines[0:4] * cosines[4:8], sines[0:4] * sines[4:8], cosines[0:4])
        shift = -(normal[0] * place[0] + normal[1] * place[1] + normal[2] * place[2])
        square = place[0] * place[0] + place[1] * place[1] + place[2] * place[2]

        def put(row, value):
            columns[pl.ds(row, POINTS, stride=64), :] = value.astype(F32)

        for axis in range(3):
            for part, value in enumerate(parts3(normal[axis])):
                put(8 * part + axis, value)
            for part, value in enumerate(parts3(place[axis])):
                put(32 + 8 * part + axis, value)
        for part, value in enumerate(parts3(shift)):
            put(24 + part, value)
        for part, value in enumerate(parts3(square)):
            put(56 + part, value)
        for point in range(POINTS):
            block = [columns[64 * point + 8 * i : 64 * point + 8 * i + 8, :] for i in range(8)]
            n1, n2, n3, c, x1, x2, x3, q = block
            both = [n1, n1, n1, n2, n2, n3, c, blank, q, x1, x1, x1, x2, x2, x3, ones]
            at = pl.ds(point * TILE, TILE)
            left_ref[slot, at, :] = jnp.concatenate(both, axis=0).astype(BF16).T
        return carry

    lax.fori_loop(0, count_ref[group], one_slot, 0)


def radiosity_of(rad_ref, spot):
    pair = rad_ref[pl.ds(2 * spot, 2), :]
    both = jnp.concatenate([pair >> 16, pair & 65535], axis=0)
    return (both.astype(F32) * (1.0 / RAD)).astype(BF16)


def slots_of_half(
    half_tiles, wanted, list_ref, count_ref, spot_ref, left_ref, centre_ref, visible_ref, rad_ref,
    points_ref, total, words, order, right, gains,
):
    group = lax.axis_index("cols")
    point_rows = 12 * half_tiles
    words[0 : point_rows + REFS, :] = points_ref[...]
    sub = lax.broadcasted_iota(jnp.int32, (8, POINTS * TILE), 0)
    valid = sub < 3
    away = points_ref[point_rows:, :].astype(F32) - centre_ref[...]
    away = jnp.concatenate([away] * POINTS, axis=1)
    blank = jnp.zeros((8, POINTS * TILE), F32)
    ones = jnp.where(valid, 1.0, 0.0).astype(F32)

    def pick(slot, found):
        order[found] = slot
        return found + (list_ref[group, 1, slot] // half_tiles == wanted).astype(jnp.int32)

    found = lax.fori_loop(0, count_ref[group], pick, 0)

    def stack3(value):
        first, second, third = (part.astype(F32) for part in parts3(value))
        return jnp.where(sub == 0, first, jnp.where(sub == 1, second, jnp.where(valid, third, 0.0)))

    def split(value):
        return [part.astype(F32) for part in parts3(value)]

    def prepare(index, which):
        start = (list_ref[group, 1, order[index]] % half_tiles) * 12
        word = jnp.concatenate(
            [words[pl.ds(start + point, 8, stride=POINTS), :] for point in range(POINTS)], axis=1
        )
        place = jnp.where(valid, (word >> 16).astype(F32) * (1.0 / POS) + away, 0.0)
        moment = jnp.where(valid, ((word << 16) >> 16).astype(F32) * (1.0 / MOM), 0.0)
        area = jnp.sqrt(jnp.sum(moment * moment, axis=0, keepdims=True))
        shift = stack3(-jnp.sum(moment * place, axis=0, keepdims=True))
        square = stack3(jnp.sum(place * place, axis=0, keepdims=True) + area)
        x1, x2, x3 = split(place)
        m1, m2, m3 = split(moment)
        y1, y2, y3 = -2.0 * x1, -2.0 * x2, -2.0 * x3
        empty = [blank] * 8
        right[which, 0] = jnp.concatenate([x1, x2, x3, x1, x2, x1, ones, blank] + empty, axis=0).astype(BF16)
        right[which, 1] = jnp.concatenate(empty + [blank, m1, m2, m3, m1, m2, m1, shift], axis=0).astype(BF16)
        right[which, 2] = jnp.concatenate(empty + [ones, y1, y2, y3, y1, y2, y1, square], axis=0).astype(BF16)

    def finish(index, which):
        slot = order[index]
        rad = radiosity_of(rad_ref, spot_ref[spot_ref.shape[0] - list_ref.shape[2] + slot])
        part = lax.dot_general(rad, gains[which, 0], NT, preferred_element_type=F32)
        part = part + lax.dot_general(rad, gains[which, 1], NT, preferred_element_type=F32)
        row = list_ref[group, 0, slot]
        total[row] = total[row] + part * (1.0 / (math.pi * POINTS))

    def make(index, which):
        slot = order[index]
        gain = None
        for pair in range(POINTS // 2):
            at = slice(2 * pair * TILE, 2 * (pair + 1) * TILE)
            left = left_ref[slot]
            facing = jnp.dot(left, right[which, 0, :, at], preferred_element_type=F32)
            toward = jnp.dot(left, right[which, 1, :, at], preferred_element_type=F32)
            spread = jnp.dot(left, right[which, 2, :, at], preferred_element_type=F32)
            over = jnp.maximum(facing, 0.0) * jnp.maximum(toward, 0.0)
            under = spread * spread
            over_a, over_b = over[:, :TILE], over[:, TILE:]
            under_a, under_b = under[:, :TILE], under[:, TILE:]
            term = (over_a * under_b + over_b * under_a) / (under_a * under_b)
            for point in range(POINTS):
                one = term[point * TILE : (point + 1) * TILE]
                gain = one if gain is None else gain + one
        return gain * visible_ref[slot].astype(F32)

    def keep(gain, which):
        high = gain.astype(BF16)
        gains[which, 0] = high
        gains[which, 1] = (gain - high.astype(F32)).astype(BF16)

    def two_slots(index, carry):
        first = 2 * index
        second = jnp.minimum(first + 1, found - 1)
        live = jnp.where(first + 1 < found, 1.0, 0.0)
        finish(jnp.maximum(first - 2, 0), 0)
        finish(jnp.maximum(first - 1, 0), 1)
        gain_a = make(first, 0)
        gain_b = make(second, 1) * live
        prepare(jnp.minimum(first + 2, found - 1), 0)
        prepare(jnp.minimum(first + 3, found - 1), 1)
        keep(gain_a, 0)
        keep(gain_b, 1)
        return carry

    @pl.when(found > 0)
    def _():
        gains[...] = jnp.zeros_like(gains)
        prepare(0, 0)
        prepare(jnp.minimum(1, found - 1), 1)
        trips = (found + 1) // 2
        lax.fori_loop(0, trips, two_slots, 0)
        finish(2 * trips - 2, 0)
        finish(jnp.minimum(2 * trips - 1, found - 1), 1)


def own_kernel(
    half_tiles, list_ref, count_ref, static_ref, spot_ref, left_ref, centre_ref,
    visible_ref, rad_ref, points_ref, tiles_hbm, total_ref, tiles, arrived, words, order, right, gains,
):
    batch = tiles.shape[0] // CHUNKS
    copies = []
    for chunk in range(CHUNKS):
        part = pl.ds(chunk * batch, batch)
        copies.append(pltpu.make_async_copy(tiles_hbm.at[part], tiles.at[part], arrived.at[chunk]))
        copies[-1].start()
    total_ref[...] = jnp.zeros_like(total_ref)
    slots_of_half(
        half_tiles, held_half(), list_ref, count_ref, spot_ref, left_ref, centre_ref,
        visible_ref, rad_ref, points_ref, total_ref, words, order, right, gains,
    )
    for chunk in range(CHUNKS):
        copies[chunk].wait()
        parts = []
        for one in range(chunk * batch, (chunk + 1) * batch):
            rad = radiosity_of(rad_ref, spot_ref[one])
            parts.append(lax.dot_general(rad, tiles[one], NT, preferred_element_type=F32))
        for step, part in enumerate(parts):
            row = static_ref[0, chunk * batch + step]
            total_ref[row] = total_ref[row] + part


def other_kernel(
    half_tiles, out_tiles, list_ref, count_ref, spot_ref, left_ref, centre_ref, visible_ref, rad_ref,
    points_ref, sum_ref, keep_ref, send_ref, total, words, order, right, gains,
):
    group = lax.axis_index("cols")
    total[...] = sum_ref[...]
    slots_of_half(
        half_tiles, 1 - held_half(), list_ref, count_ref, spot_ref, left_ref,
        centre_ref, visible_ref, rad_ref, points_ref, total, words, order, right, gains,
    )
    for tile in range(out_tiles):
        at = slice(tile * TILE, (tile + 1) * TILE)
        keep_ref[:, at] = total[group * out_tiles + tile]
        send_ref[:, at] = total[(1 - group) * out_tiles + tile]


def body(
    radiosity,
    emission,
    material,
    reflectance,
    static_tiles,
    static_index,
    row_geometry,
    array_geometry,
    array_owner,
    array_index,
    array_count,
    visibility,
):
    rows = lax.axis_size("rows")
    me = lax.axis_index("rows")
    owner = array_owner[0]
    bands, patches = radiosity.shape
    own_tiles = patches // TILE
    row_tiles = row_geometry.shape[2] // TILE
    array_tiles = array_geometry.shape[-1] // TILE
    half_tiles = array_tiles // 2
    half_rows = 12 * half_tiles + REFS
    rad_rows = 2 * own_tiles
    slots = visibility.shape[2]
    column_tiles = own_tiles * rows

    levels = rows.bit_length() - 1
    orders = hop_orders(rows)

    def hop(value, level):
        pairs = [
            (2 * row + col, 2 * (row ^ orders[col][level]) + col) for row in range(rows) for col in range(2)
        ]
        return lax.ppermute(value, ("rows", "cols"), pairs)

    def better(mine, theirs, level):
        return jnp.where(((owner ^ me) & bit_of(level, rows)) != 0, theirs, mine)

    keep, send, rad = pl.pallas_call(
        functools.partial(encode_kernel, half_tiles),
        out_shape=(
            VMEM((half_rows, TILE), jnp.int32),
            VMEM((half_rows + rad_rows, TILE), jnp.int32),
            VMEM((rad_rows, TILE), jnp.int32),
        ),
        in_specs=[whole(pltpu.HBM), whole(pltpu.HBM)],
        out_specs=(whole(), whole(), whole()),
        scratch_shapes=[
            VMEM(array_geometry.shape[2:], F32),
            VMEM(radiosity.shape, radiosity.dtype),
            pltpu.SemaphoreType.DMA((7,)),
            VMEM((2, half_rows, TILE), jnp.int32),
        ],
        compiler_params=pltpu.CompilerParams(vmem_limit_bytes=4 << 20),
        name="encode",
    )(in_hbm(array_geometry[0, 0]), in_hbm(radiosity))

    for level in range(levels):
        got = hop(send, level)
        keep = better(keep, got[:half_rows], level)
        rad = jnp.concatenate([rad, got[half_rows:]], axis=0)
        send = jnp.concatenate([keep, rad], axis=0)
    other = hop(keep, 0)

    def spot(column_tile):
        holder = (column_tile // own_tiles) ^ me
        place = jnp.zeros_like(column_tile)
        for level in range(levels):
            place = place + jnp.where((holder & bit_of(level, rows)) != 0, 1 << level, 0)
        return place * own_tiles + column_tile % own_tiles

    group = lax.axis_index("cols")
    lists = array_index[0]
    counts = array_count[0]
    static_list = static_index[0, 0]
    spots = spot(jnp.concatenate([static_list[1], column_tiles - array_tiles + lists[group, 1]]))
    smem = whole(pltpu.SMEM)
    left, centre = pl.pallas_call(
        rows_kernel,
        out_shape=(
            VMEM((slots, POINTS * TILE, TILE), BF16),
            VMEM((8, TILE), F32),
        ),
        in_specs=[smem, smem, whole(pltpu.HBM)],
        out_specs=(whole(), whole()),
        scratch_shapes=[
            VMEM(row_geometry.shape, F32),
            pltpu.SemaphoreType.DMA,
            VMEM((POINTS * 64, TILE), F32),
        ],
        compiler_params=pltpu.CompilerParams(vmem_limit_bytes=6 << 20),
        name="rows",
    )(lists, counts, in_hbm(row_geometry))

    onehot = (jnp.arange(reflectance.shape[1], dtype=jnp.int32)[:, None] == material[None, :]).astype(F32)
    albedo = jnp.dot(reflectance, onehot, precision=lax.Precision.HIGHEST)

    scratch = [
        VMEM((half_rows + 16, TILE), jnp.int32),
        pltpu.SMEM((slots,), jnp.int32),
        VMEM((2, 3, TILE, POINTS * TILE), BF16),
        VMEM((2, 2, TILE, TILE), BF16),
    ]
    params = pltpu.CompilerParams(vmem_limit_bytes=12 << 20)
    sums = pl.pallas_call(
        functools.partial(own_kernel, half_tiles),
        out_shape=VMEM((row_tiles, bands, TILE), F32),
        in_specs=[smem] * 4 + [whole()] * 5 + [whole(pltpu.HBM)],
        out_specs=whole(),
        scratch_shapes=[
            VMEM(static_tiles.shape[2:], static_tiles.dtype),
            pltpu.SemaphoreType.DMA((CHUNKS,)),
        ]
        + scratch,
        compiler_params=params,
        name="own",
    )(
        lists, counts, static_list, spots, left, centre, visibility[0, 0], rad, keep,
        in_hbm(static_tiles[0, 0]),
    )
    shape = jax.ShapeDtypeStruct((bands, patches), F32)
    kept, sent = pl.pallas_call(
        functools.partial(other_kernel, half_tiles, row_tiles // 2),
        out_shape=(shape, shape),
        in_specs=[smem] * 3 + [whole()] * 6,
        out_specs=(whole(), whole()),
        scratch_shapes=[VMEM((row_tiles, bands, TILE), F32)] + scratch,
        compiler_params=params,
        name="other",
    )(lists, counts, spots, left, centre, visibility[0, 0], rad, other, sums)
    arrived = lax.ppermute(sent, "cols", [(0, 1), (1, 0)])
    return emission + albedo * (kept + arrived)


def solution(mesh):
    in_specs = (
        P(None, ("groups", "rows", "cols")),
        P(None, ("groups", "rows", "cols")),
        P(("groups", "rows", "cols")),
        P(),
        P(("groups", "rows"), "cols", None, None, None),
        P(("groups", "rows"), "cols", None, None),
        P(None, None, ("groups", "rows")),
        P(("groups", "cols"), "rows", None, None, None),
        P(("groups", "cols")),
        P(("groups", "rows"), None, None, None),
        P(("groups", "rows"), None),
        P(("groups", "rows"), "cols", None, None, None),
    )
    out_specs = P(None, ("groups", "rows", "cols"))
    return jax.shard_map(body, mesh=mesh, in_specs=in_specs, out_specs=out_specs, check_vma=False)
```

```python
import functools
import math

import jax
import jax.numpy as jnp
from jax import lax
from jax.experimental import pallas as pl
from jax.experimental.pallas import tpu as pltpu
from jax.sharding import PartitionSpec as P

TILE = 128
POINTS = 4
POS = 2.0**14
MOM = 2.0**19
RAD = 2.0**11
BATCH = 16
REFS = 8
GROUP = 16 * 12
F32 = jnp.float32
BF16 = jnp.bfloat16
VMEM = pltpu.VMEM
NT = (((1,), (1,)), ((), ()))


def hop_orders(rows):
    high = [rows >> shift for shift in range(1, rows.bit_length() - 1)]
    return [1] + high, high + [1]


def bit_of(level, rows):
    first, second = hop_orders(rows)
    return jnp.where(lax.axis_index("cols") == 0, first[level], second[level])


def held_half():
    return ((lax.axis_index("rows") & bit_of(0, lax.axis_size("rows"))) != 0).astype(jnp.int32)


def whole(memory_space=VMEM):
    return pl.BlockSpec(memory_space=memory_space)


def in_hbm(value):
    return pltpu.with_memory_space_constraint(value, pltpu.HBM)


def parts3(value):
    first = value.astype(BF16)
    rest = value - first.astype(F32)
    second = rest.astype(BF16)
    third = (rest - second.astype(F32)).astype(BF16)
    return first, second, third


def encode_points(half_tiles, half, geo_hbm, geo_ref, arrived, out_ref):
    lanes = half_tiles * TILE
    part = pl.ds(pl.multiple_of(half * lanes, TILE), lanes)
    fields = [
        pltpu.make_async_copy(geo_hbm.at[field, :, part], geo_ref.at[field], arrived.at[field])
        for field in range(6)
    ]
    for field in (3, 4, 5, 0, 1, 2):
        fields[field].start()
    for field in (3, 4, 5):
        fields[field].wait()
    angles = jnp.concatenate([geo_ref[3], geo_ref[4]], axis=0)
    sines, cosines = jnp.sin(angles), jnp.cos(angles)
    area = geo_ref[5]
    normal = (
        sines[0:4] * cosines[4:8],
        sines[0:4] * sines[4:8],
        cosines[0:4],
    )
    point_rows = 12 * half_tiles
    for axis in range(3):
        fields[axis].wait()
        place = geo_ref[axis]
        low = jnp.min(jnp.min(place, axis=1, keepdims=True), axis=0, keepdims=True)
        high = jnp.max(jnp.max(place, axis=1, keepdims=True), axis=0, keepdims=True)
        centre = jnp.floor((low + high) * 0.5 + 0.5)
        moved = jnp.floor((place - centre) * POS + 0.5).astype(jnp.int32)
        moved = jnp.clip(moved, -32768, 32767)
        moment = jnp.floor(area * normal[axis] * MOM + 0.5).astype(jnp.int32)
        moment = jnp.clip(moment, -32768, 32767)
        words = (moved << 16) | (moment & 65535)
        for tile in range(half_tiles):
            row = 12 * tile + 4 * axis
            out_ref[row : row + 4, :] = words[:, tile * TILE : (tile + 1) * TILE]
        row = point_rows + axis
        out_ref[row : row + 1, :] = jnp.broadcast_to(centre.astype(jnp.int32), (1, TILE))
    out_ref[point_rows + 3 : point_rows + REFS, :] = jnp.zeros((REFS - 3, TILE), jnp.int32)


def send_kernel(half_tiles, geo_hbm, rad_hbm, send_ref, words_ref, geo_ref, rad_ref, arrived):
    own_rad = pltpu.make_async_copy(rad_hbm, rad_ref, arrived.at[6])
    own_rad.start()
    encode_points(half_tiles, 1 - held_half(), geo_hbm, geo_ref, arrived, send_ref)
    own_rad.wait()
    rad = (rad_ref[...].astype(F32) * RAD).astype(jnp.int32)
    rad = (rad[0:2] << 16) | rad[2:4]
    for tile in range(rad.shape[1] // TILE):
        words_ref[2 * tile : 2 * tile + 2, :] = rad[:, tile * TILE : (tile + 1) * TILE]
    send_ref[12 * half_tiles + REFS :, :] = words_ref[...]


def keep_kernel(half_tiles, geo_hbm, row_hbm, keep_ref, row_ref, geo_ref, arrived):
    rows = pltpu.make_async_copy(row_hbm, row_ref, arrived.at[6])
    rows.start()
    encode_points(half_tiles, held_half(), geo_hbm, geo_ref, arrived, keep_ref)
    rows.wait()


def rows_kernel(low, high, list_ref, count_ref, geo_ref, after, *refs):
    left_ref, centre_ref, columns = refs[-3:]
    group = lax.axis_index("cols")
    columns[...] = jnp.zeros_like(columns)
    lane_row = lax.broadcasted_iota(jnp.int32, (8, TILE), 0)
    ones = jnp.where(lane_row < 3, 1.0, 0.0).astype(F32)
    blank = jnp.zeros((8, TILE), F32)
    centre_ref[...] = blank
    centre = []
    for axis in range(3):
        first = jnp.floor(geo_ref[axis, 0:1, 0:1] + 0.5)
        centre.append(first)
        centre_ref[axis : axis + 1, :] = jnp.broadcast_to(first, (1, TILE))

    def one_slot(slot, carry):
        start = pl.multiple_of(list_ref[group, 0, slot] * TILE, TILE)
        slab = [geo_ref[field, :, pl.ds(start, TILE)] for field in range(5)]
        place = [slab[axis] - centre[axis] for axis in range(3)]
        angles = jnp.concatenate([slab[3], slab[4]], axis=0)
        sines, cosines = jnp.sin(angles), jnp.cos(angles)
        normal = (sines[0:4] * cosines[4:8], sines[0:4] * sines[4:8], cosines[0:4])
        shift = -(normal[0] * place[0] + normal[1] * place[1] + normal[2] * place[2])
        square = place[0] * place[0] + place[1] * place[1] + place[2] * place[2]

        def put(row, value):
            columns[pl.ds(row, POINTS, stride=64), :] = value.astype(F32)

        for axis in range(3):
            for part, value in enumerate(parts3(normal[axis])):
                put(8 * part + axis, value)
            for part, value in enumerate(parts3(place[axis])):
                put(32 + 8 * part + axis, value)
        for part, value in enumerate(parts3(shift)):
            put(24 + part, value)
        for part, value in enumerate(parts3(square)):
            put(56 + part, value)
        for point in range(POINTS):
            block = [columns[64 * point + 8 * i : 64 * point + 8 * i + 8, :] for i in range(8)]
            n1, n2, n3, c, x1, x2, x3, q = block
            both = [n1, n1, n1, n2, n2, n3, c, blank, q, x1, x1, x1, x2, x2, x3, ones]
            at = pl.ds(point * TILE, TILE)
            left_ref[slot, at, :] = jnp.concatenate(both, axis=0).astype(BF16).T
        return carry

    lax.fori_loop(low, jnp.minimum(count_ref[group], high), one_slot, 0)


def radiosity_of(rad_ref, spot):
    pair = rad_ref[pl.ds(2 * spot, 2), :]
    both = jnp.concatenate([pair >> 16, pair & 65535], axis=0)
    return (both.astype(F32) * (1.0 / RAD)).astype(BF16)


def slots_of_half(
    half_tiles, wanted, list_ref, count_ref, spot_ref, left_ref, centre_ref, visible_ref, rad_ref,
    points_ref, total, words, order, right, gains,
):
    group = lax.axis_index("cols")
    point_rows = 12 * half_tiles
    words[0 : point_rows + REFS, :] = points_ref[...]
    sub = lax.broadcasted_iota(jnp.int32, (8, POINTS * TILE), 0)
    valid = sub < 3
    away = points_ref[point_rows:, :].astype(F32) - centre_ref[...]
    away = jnp.concatenate([away] * POINTS, axis=1)
    blank = jnp.zeros((8, POINTS * TILE), F32)
    ones = jnp.where(valid, 1.0, 0.0).astype(F32)

    def pick(slot, found):
        order[found] = slot
        return found + (list_ref[group, 1, slot] // half_tiles == wanted).astype(jnp.int32)

    found = lax.fori_loop(0, count_ref[group], pick, 0)

    def stack3(value):
        first, second, third = (part.astype(F32) for part in parts3(value))
        return jnp.where(sub == 0, first, jnp.where(sub == 1, second, jnp.where(valid, third, 0.0)))

    def split(value):
        return [part.astype(F32) for part in parts3(value)]

    def prepare(index, which):
        start = (list_ref[group, 1, order[index]] % half_tiles) * 12
        word = jnp.concatenate(
            [words[pl.ds(start + point, 8, stride=POINTS), :] for point in range(POINTS)], axis=1
        )
        place = jnp.where(valid, (word >> 16).astype(F32) * (1.0 / POS) + away, 0.0)
        moment = jnp.where(valid, ((word << 16) >> 16).astype(F32) * (1.0 / MOM), 0.0)
        area = jnp.sqrt(jnp.sum(moment * moment, axis=0, keepdims=True))
        shift = stack3(-jnp.sum(moment * place, axis=0, keepdims=True))
        square = stack3(jnp.sum(place * place, axis=0, keepdims=True) + area)
        x1, x2, x3 = split(place)
        m1, m2, m3 = split(moment)
        y1, y2, y3 = -2.0 * x1, -2.0 * x2, -2.0 * x3
        empty = [blank] * 8
        right[which, 0] = jnp.concatenate([x1, x2, x3, x1, x2, x1, ones, blank] + empty, axis=0).astype(BF16)
        right[which, 1] = jnp.concatenate(empty + [blank, m1, m2, m3, m1, m2, m1, shift], axis=0).astype(BF16)
        right[which, 2] = jnp.concatenate(empty + [ones, y1, y2, y3, y1, y2, y1, square], axis=0).astype(BF16)

    def finish(index, which):
        slot = order[index]
        rad = radiosity_of(rad_ref, spot_ref[spot_ref.shape[0] - list_ref.shape[2] + slot])
        part = lax.dot_general(rad, gains[which, 0], NT, preferred_element_type=F32)
        part = part + lax.dot_general(rad, gains[which, 1], NT, preferred_element_type=F32)
        row = list_ref[group, 0, slot]
        total[row] = total[row] + part * (1.0 / (math.pi * POINTS))

    def make(index, which):
        slot = order[index]
        gain = None
        for pair in range(POINTS // 2):
            at = slice(2 * pair * TILE, 2 * (pair + 1) * TILE)
            left = left_ref[slot]
            facing = jnp.dot(left, right[which, 0, :, at], preferred_element_type=F32)
            toward = jnp.dot(left, right[which, 1, :, at], preferred_element_type=F32)
            spread = jnp.dot(left, right[which, 2, :, at], preferred_element_type=F32)
            over = jnp.maximum(facing, 0.0) * jnp.maximum(toward, 0.0)
            under = spread * spread
            over_a, over_b = over[:, :TILE], over[:, TILE:]
            under_a, under_b = under[:, :TILE], under[:, TILE:]
            term = (over_a * under_b + over_b * under_a) / (under_a * under_b)
            for point in range(POINTS):
                one = term[point * TILE : (point + 1) * TILE]
                gain = one if gain is None else gain + one
        return gain * visible_ref[slot].astype(F32)

    def keep(gain, which):
        high = gain.astype(BF16)
        gains[which, 0] = high
        gains[which, 1] = (gain - high.astype(F32)).astype(BF16)

    def two_slots(index, carry):
        first = 2 * index
        second = jnp.minimum(first + 1, found - 1)
        live = jnp.where(first + 1 < found, 1.0, 0.0)
        finish(jnp.maximum(first - 2, 0), 0)
        finish(jnp.maximum(first - 1, 0), 1)
        gain_a = make(first, 0)
        gain_b = make(second, 1) * live
        prepare(jnp.minimum(first + 2, found - 1), 0)
        prepare(jnp.minimum(first + 3, found - 1), 1)
        keep(gain_a, 0)
        keep(gain_b, 1)
        return carry

    @pl.when(found > 0)
    def _():
        gains[...] = jnp.zeros_like(gains)
        prepare(0, 0)
        prepare(jnp.minimum(1, found - 1), 1)
        trips = (found + 1) // 2
        lax.fori_loop(0, trips, two_slots, 0)
        finish(2 * trips - 2, 0)
        finish(jnp.minimum(2 * trips - 1, found - 1), 1)


def own_kernel(
    half_tiles, list_ref, count_ref, static_ref, spot_ref, left_ref, centre_ref,
    visible_ref, rad_ref, points_ref, tiles_hbm, total_ref, tiles, arrived, words, order, right, gains,
):
    copy = pltpu.make_async_copy(tiles_hbm, tiles, arrived)
    copy.start()
    total_ref[...] = jnp.zeros_like(total_ref)
    slots_of_half(
        half_tiles, held_half(), list_ref, count_ref, spot_ref, left_ref, centre_ref,
        visible_ref, rad_ref, points_ref, total_ref, words, order, right, gains,
    )
    copy.wait()
    for first in range(0, tiles.shape[0], BATCH):
        parts = []
        for one in range(first, first + BATCH):
            rad = radiosity_of(rad_ref, spot_ref[one])
            parts.append(lax.dot_general(rad, tiles[one], NT, preferred_element_type=F32))
        for step, part in enumerate(parts):
            row = static_ref[0, first + step]
            total_ref[row] = total_ref[row] + part


def other_kernel(
    half_tiles, out_tiles, list_ref, count_ref, spot_ref, left_ref, centre_ref, visible_ref, rad_ref,
    points_ref, sum_ref, keep_ref, send_ref, total, words, order, right, gains,
):
    group = lax.axis_index("cols")
    total[...] = sum_ref[...]
    slots_of_half(
        half_tiles, 1 - held_half(), list_ref, count_ref, spot_ref, left_ref,
        centre_ref, visible_ref, rad_ref, points_ref, total, words, order, right, gains,
    )
    for tile in range(out_tiles):
        at = slice(tile * TILE, (tile + 1) * TILE)
        keep_ref[:, at] = total[group * out_tiles + tile]
        send_ref[:, at] = total[(1 - group) * out_tiles + tile]


def body(
    radiosity,
    emission,
    material,
    reflectance,
    static_tiles,
    static_index,
    row_geometry,
    array_geometry,
    array_owner,
    array_index,
    array_count,
    visibility,
):
    rows = lax.axis_size("rows")
    me = lax.axis_index("rows")
    owner = array_owner[0]
    bands, patches = radiosity.shape
    own_tiles = patches // TILE
    row_tiles = row_geometry.shape[2] // TILE
    array_tiles = array_geometry.shape[-1] // TILE
    half_tiles = array_tiles // 2
    half_rows = 12 * half_tiles + REFS
    rad_rows = 2 * own_tiles
    slots = visibility.shape[2]
    column_tiles = own_tiles * rows

    levels = rows.bit_length() - 1
    orders = hop_orders(rows)

    def hop(value, level):
        pairs = [
            (2 * row + col, 2 * (row ^ orders[col][level]) + col) for row in range(rows) for col in range(2)
        ]
        return lax.ppermute(value, ("rows", "cols"), pairs)

    def better(mine, theirs, level):
        return jnp.where(((owner ^ me) & bit_of(level, rows)) != 0, theirs, mine)

    half_shape = (*array_geometry.shape[2:4], half_tiles * TILE)
    candidates = in_hbm(array_geometry[0, 0])
    hbm = whole(pltpu.HBM)
    small = pltpu.CompilerParams(vmem_limit_bytes=4 << 20)
    send, rad = pl.pallas_call(
        functools.partial(send_kernel, half_tiles),
        out_shape=(VMEM((half_rows + rad_rows, TILE), jnp.int32), VMEM((rad_rows, TILE), jnp.int32)),
        in_specs=[hbm, hbm],
        out_specs=(whole(), whole()),
        scratch_shapes=[
            VMEM(half_shape, F32),
            VMEM(radiosity.shape, radiosity.dtype),
            pltpu.SemaphoreType.DMA((7,)),
        ],
        compiler_params=small,
        name="send",
    )(candidates, in_hbm(radiosity))
    keep, geometry = pl.pallas_call(
        functools.partial(keep_kernel, half_tiles),
        out_shape=(VMEM((half_rows, TILE), jnp.int32), VMEM(row_geometry.shape, F32)),
        in_specs=[hbm, hbm],
        out_specs=(whole(), whole()),
        scratch_shapes=[VMEM(half_shape, F32), pltpu.SemaphoreType.DMA((7,))],
        compiler_params=small,
        name="keep",
    )(candidates, in_hbm(row_geometry))
    smem = whole(pltpu.SMEM)
    lists = array_index[0]
    counts = array_count[0]

    def rows_call(low, high, after, *so_far):
        return pl.pallas_call(
            functools.partial(rows_kernel, low, high),
            out_shape=(VMEM((slots, POINTS * TILE, TILE), BF16), VMEM((8, TILE), F32)),
            in_specs=[smem, smem, whole(), whole(pl.ANY)] + [whole()] * len(so_far),
            out_specs=(whole(), whole()),
            input_output_aliases={4: 0, 5: 1} if so_far else {},
            scratch_shapes=[VMEM((POINTS * 64, TILE), F32)],
            compiler_params=small,
            name="rows_low" if low == 0 else "rows_high",
        )(lists, counts, geometry, after, *so_far)

    for level in range(levels):
        got = hop(send, level)
        if level == 1:
            left, centre = rows_call(0, slots // 2, keep)
            got, left = lax.optimization_barrier((got, left))
        keep = better(keep, got[:half_rows], level)
        rad = jnp.concatenate([rad, got[half_rows:]], axis=0)
        send = jnp.concatenate([keep, rad], axis=0)
        if level == 1:
            left, centre = rows_call(slots // 2, slots, keep, left, centre)
    other = hop(keep, 0)

    def spot(column_tile):
        holder = (column_tile // own_tiles) ^ me
        place = jnp.zeros_like(column_tile)
        for level in range(levels):
            place = place + jnp.where((holder & bit_of(level, rows)) != 0, 1 << level, 0)
        return place * own_tiles + column_tile % own_tiles

    group = lax.axis_index("cols")
    static_list = static_index[0, 0]
    spots = spot(jnp.concatenate([static_list[1], column_tiles - array_tiles + lists[group, 1]]))
    onehot = (jnp.arange(reflectance.shape[1], dtype=jnp.int32)[:, None] == material[None, :]).astype(F32)
    albedo = jnp.dot(reflectance, onehot, precision=lax.Precision.HIGHEST)

    scratch = [
        VMEM((half_rows + 16, TILE), jnp.int32),
        pltpu.SMEM((slots,), jnp.int32),
        VMEM((2, 3, TILE, POINTS * TILE), BF16),
        VMEM((2, 2, TILE, TILE), BF16),
    ]
    params = pltpu.CompilerParams(vmem_limit_bytes=12 << 20)
    sums = pl.pallas_call(
        functools.partial(own_kernel, half_tiles),
        out_shape=VMEM((row_tiles, bands, TILE), F32),
        in_specs=[smem] * 4 + [whole()] * 5 + [whole(pltpu.HBM)],
        out_specs=whole(),
        scratch_shapes=[
            VMEM(static_tiles.shape[2:], static_tiles.dtype),
            pltpu.SemaphoreType.DMA,
        ]
        + scratch,
        compiler_params=params,
        name="own",
    )(
        lists, counts, static_list, spots, left, centre, visibility[0, 0], rad, keep,
        in_hbm(static_tiles[0, 0]),
    )
    shape = jax.ShapeDtypeStruct((bands, patches), F32)
    mine, sent = pl.pallas_call(
        functools.partial(other_kernel, half_tiles, row_tiles // 2),
        out_shape=(shape, shape),
        in_specs=[smem] * 3 + [whole()] * 6,
        out_specs=(whole(), whole()),
        scratch_shapes=[VMEM((row_tiles, bands, TILE), F32)] + scratch,
        compiler_params=params,
        name="other",
    )(lists, counts, spots, left, centre, visibility[0, 0], rad, other, sums)
    arrived = lax.ppermute(sent, "cols", [(0, 1), (1, 0)])
    return emission + albedo * (mine + arrived)


def solution(mesh):
    in_specs = (
        P(None, ("groups", "rows", "cols")),
        P(None, ("groups", "rows", "cols")),
        P(("groups", "rows", "cols")),
        P(),
        P(("groups", "rows"), "cols", None, None, None),
        P(("groups", "rows"), "cols", None, None),
        P(None, None, ("groups", "rows")),
        P(("groups", "cols"), "rows", None, None, None),
        P(("groups", "cols")),
        P(("groups", "rows"), None, None, None),
        P(("groups", "rows"), None),
        P(("groups", "rows"), "cols", None, None, None),
    )
    out_specs = P(None, ("groups", "rows", "cols"))
    return jax.shard_map(body, mesh=mesh, in_specs=in_specs, out_specs=out_specs, check_vma=False)
```

```python
import functools
import math

import jax
import jax.numpy as jnp
from jax import lax
from jax.experimental import pallas as pl
from jax.experimental.pallas import tpu as pltpu
from jax.sharding import PartitionSpec as P

TILE = 128
POINTS = 4
POS = 2.0**13
MOM = 2.0**19
RAD = 2.0**11
BATCH = 16
REFS = 8
GROUP = 16 * 12
F32 = jnp.float32
BF16 = jnp.bfloat16
VMEM = pltpu.VMEM
NT = (((1,), (1,)), ((), ()))


def hop_orders(rows):
    high = [rows >> shift for shift in range(1, rows.bit_length() - 1)]
    return high + [1], high[1:] + high[:1] + [1]


def bit_of(level, rows):
    first, second = hop_orders(rows)
    return jnp.where(lax.axis_index("cols") == 0, first[level], second[level])


def held_half():
    return ((lax.axis_index("rows") & bit_of(0, lax.axis_size("rows"))) != 0).astype(jnp.int32)


def whole(memory_space=VMEM):
    return pl.BlockSpec(memory_space=memory_space)


def in_hbm(value):
    return pltpu.with_memory_space_constraint(value, pltpu.HBM)


def parts3(value):
    first = value.astype(BF16)
    rest = value - first.astype(F32)
    second = rest.astype(BF16)
    third = (rest - second.astype(F32)).astype(BF16)
    return first, second, third


def encode_points(half_tiles, half, geo_hbm, geo_ref, arrived, out_ref):
    lanes = half_tiles * TILE
    part = pl.ds(pl.multiple_of(half * lanes, TILE), lanes)
    fields = [
        pltpu.make_async_copy(geo_hbm.at[field, :, part], geo_ref.at[field], arrived.at[field])
        for field in range(6)
    ]
    for field in (3, 4, 5, 0, 1, 2):
        fields[field].start()
    for field in (3, 4, 5):
        fields[field].wait()
    angles = jnp.concatenate([geo_ref[3], geo_ref[4]], axis=0)
    sines, cosines = jnp.sin(angles), jnp.cos(angles)
    area = geo_ref[5]
    normal = (
        sines[0:4] * cosines[4:8],
        sines[0:4] * sines[4:8],
        cosines[0:4],
    )
    point_rows = 12 * half_tiles
    for axis in range(3):
        fields[axis].wait()
        place = geo_ref[axis]
        centre = jnp.floor(place[0:1, 0:1] + 0.5)
        moved = jnp.floor((place - centre) * POS + 0.5).astype(jnp.int32)
        moved = jnp.clip(moved, -32768, 32767)
        moment = jnp.floor(area * normal[axis] * MOM + 0.5).astype(jnp.int32)
        moment = jnp.clip(moment, -32768, 32767)
        words = (moved << 16) | (moment & 65535)
        for tile in range(half_tiles):
            row = 12 * tile + 4 * axis
            out_ref[row : row + 4, :] = words[:, tile * TILE : (tile + 1) * TILE]
        row = point_rows + axis
        out_ref[row : row + 1, :] = jnp.broadcast_to(centre.astype(jnp.int32), (1, TILE))
    out_ref[point_rows + 3 : point_rows + REFS, :] = jnp.zeros((REFS - 3, TILE), jnp.int32)


def send_kernel(half_tiles, geo_hbm, rad_hbm, send_ref, words_ref, geo_ref, rad_ref, arrived):
    own_rad = pltpu.make_async_copy(rad_hbm, rad_ref, arrived.at[6])
    own_rad.start()
    encode_points(half_tiles, 1 - held_half(), geo_hbm, geo_ref, arrived, send_ref)
    own_rad.wait()
    rad = (rad_ref[...].astype(F32) * RAD).astype(jnp.int32)
    rad = (rad[0:2] << 16) | rad[2:4]
    for tile in range(rad.shape[1] // TILE):
        words_ref[2 * tile : 2 * tile + 2, :] = rad[:, tile * TILE : (tile + 1) * TILE]
    send_ref[12 * half_tiles + REFS :, :] = words_ref[...]


def keep_kernel(half_tiles, geo_hbm, row_hbm, keep_ref, row_ref, geo_ref, arrived):
    rows = pltpu.make_async_copy(row_hbm, row_ref, arrived.at[6])
    rows.start()
    encode_points(half_tiles, held_half(), geo_hbm, geo_ref, arrived, keep_ref)
    rows.wait()


def rows_kernel(low, high, list_ref, count_ref, geo_ref, after, *refs):
    left_ref, centre_ref, columns = refs[-3:]
    group = lax.axis_index("cols")
    columns[...] = jnp.zeros_like(columns)
    lane_row = lax.broadcasted_iota(jnp.int32, (8, TILE), 0)
    ones = jnp.where(lane_row < 3, 1.0, 0.0).astype(F32)
    blank = jnp.zeros((8, TILE), F32)
    centre_ref[...] = blank
    centre = []
    for axis in range(3):
        first = jnp.floor(geo_ref[axis, 0:1, 0:1] + 0.5)
        centre.append(first)
        centre_ref[axis : axis + 1, :] = jnp.broadcast_to(first, (1, TILE))

    def one_slot(slot, carry):
        start = pl.multiple_of(list_ref[group, 0, slot] * TILE, TILE)
        slab = [geo_ref[field, :, pl.ds(start, TILE)] for field in range(5)]
        place = [slab[axis] - centre[axis] for axis in range(3)]
        angles = jnp.concatenate([slab[3], slab[4]], axis=0)
        sines, cosines = jnp.sin(angles), jnp.cos(angles)
        normal = (sines[0:4] * cosines[4:8], sines[0:4] * sines[4:8], cosines[0:4])
        shift = -(normal[0] * place[0] + normal[1] * place[1] + normal[2] * place[2])
        square = place[0] * place[0] + place[1] * place[1] + place[2] * place[2]

        def put(row, value):
            columns[pl.ds(row, POINTS, stride=64), :] = value.astype(F32)

        for axis in range(3):
            for part, value in enumerate(parts3(normal[axis])):
                put(8 * part + axis, value)
            for part, value in enumerate(parts3(place[axis])):
                put(32 + 8 * part + axis, value)
        for part, value in enumerate(parts3(shift)):
            put(24 + part, value)
        for part, value in enumerate(parts3(square)):
            put(56 + part, value)
        for point in range(POINTS):
            block = [columns[64 * point + 8 * i : 64 * point + 8 * i + 8, :] for i in range(8)]
            n1, n2, n3, c, x1, x2, x3, q = block
            both = [n1, n1, n1, n2, n2, n3, c, blank, q, x1, x1, x1, x2, x2, x3, ones]
            at = pl.ds(point * TILE, TILE)
            left_ref[slot, at, :] = jnp.concatenate(both, axis=0).astype(BF16).T
        return carry

    lax.fori_loop(low, jnp.minimum(count_ref[group], high), one_slot, 0)


def radiosity_of(rad_ref, spot):
    pair = rad_ref[pl.ds(2 * spot, 2), :]
    both = jnp.concatenate([pair >> 16, pair & 65535], axis=0)
    return (both.astype(F32) * (1.0 / RAD)).astype(BF16)


def slots_of_half(
    half_tiles, last_half, list_ref, count_ref, spot_ref, left_ref, centre_ref, visible_ref, rad_ref,
    points, total, words, away, order, right, gains,
):
    group = lax.axis_index("cols")
    held = held_half()
    point_rows = 12 * half_tiles
    sub = lax.broadcasted_iota(jnp.int32, (8, POINTS * TILE), 0)
    valid = sub < 3
    for half, points_ref in enumerate(points):
        words[half, 0 : point_rows + REFS, :] = points_ref[...]
        apart = points_ref[point_rows:, :].astype(F32) - centre_ref[...]
        away[half] = jnp.concatenate([apart] * POINTS, axis=1)
    blank = jnp.zeros((8, POINTS * TILE), F32)
    ones = jnp.where(valid, 1.0, 0.0).astype(F32)

    def half_of(slot):
        return (list_ref[group, 1, slot] // half_tiles) ^ held

    def pick(slot, seen):
        found, odd = seen
        late = half_of(slot)
        order[jnp.where(late == int(last_half), found, order.shape[0] - 1)] = slot
        return found + (late == int(last_half)).astype(jnp.int32), jnp.where(late == 0, slot, odd)

    count = count_ref[group]
    found, latest = lax.fori_loop(0, count, pick, (jnp.int32(0), jnp.int32(0)))
    if last_half:
        spare = (count - found) % 2
        order[jnp.where(spare == 1, found, order.shape[0] - 1)] = latest
        found = found + spare
    else:
        found = found - found % 2

    def stack3(value):
        first, second, third = (part.astype(F32) for part in parts3(value))
        return jnp.where(sub == 0, first, jnp.where(sub == 1, second, jnp.where(valid, third, 0.0)))

    def split(value):
        return [part.astype(F32) for part in parts3(value)]

    def prepare(index, which):
        slot = order[index]
        half = half_of(slot) if last_half else 0
        start = (list_ref[group, 1, slot] % half_tiles) * 12
        word = jnp.concatenate(
            [words[half, pl.ds(start + point, 8, stride=POINTS), :] for point in range(POINTS)], axis=1
        )
        place = jnp.where(valid, (word >> 16).astype(F32) * (1.0 / POS) + away[half], 0.0)
        moment = jnp.where(valid, ((word << 16) >> 16).astype(F32) * (1.0 / MOM), 0.0)
        area = jnp.sqrt(jnp.sum(moment * moment, axis=0, keepdims=True))
        shift = stack3(-jnp.sum(moment * place, axis=0, keepdims=True))
        square = stack3(jnp.sum(place * place, axis=0, keepdims=True) + area)
        x1, x2, x3 = split(place)
        m1, m2, m3 = split(moment)
        y1, y2, y3 = -2.0 * x1, -2.0 * x2, -2.0 * x3
        empty = [blank] * 8
        right[which, 0] = jnp.concatenate([x1, x2, x3, x1, x2, x1, ones, blank] + empty, axis=0).astype(BF16)
        right[which, 1] = jnp.concatenate(empty + [blank, m1, m2, m3, m1, m2, m1, shift], axis=0).astype(BF16)
        right[which, 2] = jnp.concatenate(empty + [ones, y1, y2, y3, y1, y2, y1, square], axis=0).astype(BF16)

    def finish(index, which):
        slot = order[index]
        rad = radiosity_of(rad_ref, spot_ref[spot_ref.shape[0] - list_ref.shape[2] + slot])
        part = lax.dot_general(rad, gains[which, 0], NT, preferred_element_type=F32)
        part = part + lax.dot_general(rad, gains[which, 1], NT, preferred_element_type=F32)
        row = list_ref[group, 0, slot]
        total[row] = total[row] + part * (1.0 / (math.pi * POINTS))

    def make(index, which):
        slot = order[index]
        gain = None
        for pair in range(POINTS // 2):
            at = slice(2 * pair * TILE, 2 * (pair + 1) * TILE)
            left = left_ref[slot]
            facing = jnp.dot(left, right[which, 0, :, at], preferred_element_type=F32)
            toward = jnp.dot(left, right[which, 1, :, at], preferred_element_type=F32)
            spread = jnp.dot(left, right[which, 2, :, at], preferred_element_type=F32)
            over = jnp.maximum(facing, 0.0) * jnp.maximum(toward, 0.0)
            under = spread * spread
            over_a, over_b = over[:, :TILE], over[:, TILE:]
            under_a, under_b = under[:, :TILE], under[:, TILE:]
            term = (over_a * under_b + over_b * under_a) / (under_a * under_b)
            for point in range(POINTS):
                one = term[point * TILE : (point + 1) * TILE]
                gain = one if gain is None else gain + one
        return gain * visible_ref[slot].astype(F32)

    def keep(gain, which):
        high = gain.astype(BF16)
        gains[which, 0] = high
        gains[which, 1] = (gain - high.astype(F32)).astype(BF16)

    def two_slots(index, carry):
        first = 2 * index
        second = jnp.minimum(first + 1, found - 1)
        live = jnp.where(first + 1 < found, 1.0, 0.0)
        finish(jnp.maximum(first - 2, 0), 0)
        finish(jnp.maximum(first - 1, 0), 1)
        gain_a = make(first, 0)
        gain_b = make(second, 1) * live
        prepare(jnp.minimum(first + 2, found - 1), 0)
        prepare(jnp.minimum(first + 3, found - 1), 1)
        keep(gain_a, 0)
        keep(gain_b, 1)
        return carry

    @pl.when(found > 0)
    def _():
        gains[...] = jnp.zeros_like(gains)
        prepare(0, 0)
        prepare(jnp.minimum(1, found - 1), 1)
        trips = (found + 1) // 2
        lax.fori_loop(0, trips, two_slots, 0)
        finish(2 * trips - 2, 0)
        finish(jnp.minimum(2 * trips - 1, found - 1), 1)


def own_kernel(
    half_tiles, list_ref, count_ref, static_ref, spot_ref, left_ref, centre_ref,
    visible_ref, rad_ref, points_ref, tiles_hbm, total_ref, tiles, arrived, words, away, order, right, gains,
):
    copy = pltpu.make_async_copy(tiles_hbm, tiles, arrived)
    copy.start()
    total_ref[...] = jnp.zeros_like(total_ref)
    slots_of_half(
        half_tiles, False, list_ref, count_ref, spot_ref, left_ref, centre_ref,
        visible_ref, rad_ref, [points_ref], total_ref, words, away, order, right, gains,
    )
    copy.wait()
    for first in range(0, tiles.shape[0], BATCH):
        parts = []
        for one in range(first, first + BATCH):
            rad = radiosity_of(rad_ref, spot_ref[one])
            parts.append(lax.dot_general(rad, tiles[one], NT, preferred_element_type=F32))
        for step, part in enumerate(parts):
            row = static_ref[0, first + step]
            total_ref[row] = total_ref[row] + part


def other_kernel(
    half_tiles, out_tiles, list_ref, count_ref, spot_ref, left_ref, centre_ref, visible_ref, rad_ref,
    own_ref, points_ref, sum_ref, keep_ref, send_ref, total, words, away, order, right, gains,
):
    group = lax.axis_index("cols")
    total[...] = sum_ref[...]
    slots_of_half(
        half_tiles, True, list_ref, count_ref, spot_ref, left_ref, centre_ref,
        visible_ref, rad_ref, [own_ref, points_ref], total, words, away, order, right, gains,
    )
    for tile in range(out_tiles):
        at = slice(tile * TILE, (tile + 1) * TILE)
        keep_ref[:, at] = total[group * out_tiles + tile]
        send_ref[:, at] = total[(1 - group) * out_tiles + tile]


def body(
    radiosity,
    emission,
    material,
    reflectance,
    static_tiles,
    static_index,
    row_geometry,
    array_geometry,
    array_owner,
    array_index,
    array_count,
    visibility,
):
    rows = lax.axis_size("rows")
    me = lax.axis_index("rows")
    owner = array_owner[0]
    bands, patches = radiosity.shape
    own_tiles = patches // TILE
    row_tiles = row_geometry.shape[2] // TILE
    array_tiles = array_geometry.shape[-1] // TILE
    half_tiles = array_tiles // 2
    half_rows = 12 * half_tiles + REFS
    rad_rows = 2 * own_tiles
    slots = visibility.shape[2]
    column_tiles = own_tiles * rows

    levels = rows.bit_length() - 1
    orders = hop_orders(rows)

    def hop(value, level):
        pairs = [
            (2 * row + col, 2 * (row ^ orders[col][level]) + col) for row in range(rows) for col in range(2)
        ]
        return lax.ppermute(value, ("rows", "cols"), pairs)

    def better(mine, theirs, level):
        return jnp.where(((owner ^ me) & bit_of(level, rows)) != 0, theirs, mine)

    half_shape = (*array_geometry.shape[2:4], half_tiles * TILE)
    candidates = in_hbm(array_geometry[0, 0])
    hbm = whole(pltpu.HBM)
    small = pltpu.CompilerParams(vmem_limit_bytes=4 << 20)
    send, rad = pl.pallas_call(
        functools.partial(send_kernel, half_tiles),
        out_shape=(VMEM((half_rows + rad_rows, TILE), jnp.int32), VMEM((rad_rows, TILE), jnp.int32)),
        in_specs=[hbm, hbm],
        out_specs=(whole(), whole()),
        scratch_shapes=[
            VMEM(half_shape, F32),
            VMEM(radiosity.shape, radiosity.dtype),
            pltpu.SemaphoreType.DMA((7,)),
        ],
        compiler_params=small,
        name="send",
    )(candidates, in_hbm(radiosity))
    keep, geometry = pl.pallas_call(
        functools.partial(keep_kernel, half_tiles),
        out_shape=(VMEM((half_rows, TILE), jnp.int32), VMEM(row_geometry.shape, F32)),
        in_specs=[hbm, hbm],
        out_specs=(whole(), whole()),
        scratch_shapes=[VMEM(half_shape, F32), pltpu.SemaphoreType.DMA((7,))],
        compiler_params=small,
        name="keep",
    )(candidates, in_hbm(row_geometry))
    smem = whole(pltpu.SMEM)
    lists = array_index[0]
    counts = array_count[0]

    def rows_call(low, high, after, *so_far):
        return pl.pallas_call(
            functools.partial(rows_kernel, low, high),
            out_shape=(VMEM((slots, POINTS * TILE, TILE), BF16), VMEM((8, TILE), F32)),
            in_specs=[smem, smem, whole(), whole(pl.ANY)] + [whole()] * len(so_far),
            out_specs=(whole(), whole()),
            input_output_aliases={4: 0, 5: 1} if so_far else {},
            scratch_shapes=[VMEM((POINTS * 64, TILE), F32)],
            compiler_params=small,
            name="rows_low" if low == 0 else "rows_high",
        )(lists, counts, geometry, after, *so_far)

    for level in range(levels):
        got = hop(send, level)
        if level == 1:
            left, centre = rows_call(0, slots // 2, keep)
            got, left = lax.optimization_barrier((got, left))
        keep = better(keep, got[:half_rows], level)
        rad = jnp.concatenate([rad, got[half_rows:]], axis=0)
        send = jnp.concatenate([keep, rad], axis=0)
        if level == 1:
            left, centre = rows_call(slots // 2, slots, keep, left, centre)
    other = hop(keep, 0)

    def spot(column_tile):
        holder = (column_tile // own_tiles) ^ me
        place = jnp.zeros_like(column_tile)
        for level in range(levels):
            place = place + jnp.where((holder & bit_of(level, rows)) != 0, 1 << level, 0)
        return place * own_tiles + column_tile % own_tiles

    group = lax.axis_index("cols")
    static_list = static_index[0, 0]
    spots = spot(jnp.concatenate([static_list[1], column_tiles - array_tiles + lists[group, 1]]))
    onehot = (jnp.arange(reflectance.shape[1], dtype=jnp.int32)[:, None] == material[None, :]).astype(F32)
    albedo = jnp.dot(reflectance, onehot, precision=lax.Precision.HIGHEST)

    scratch = [
        VMEM((2, half_rows + 16, TILE), jnp.int32),
        VMEM((2, 8, POINTS * TILE), F32),
        pltpu.SMEM((slots + 1,), jnp.int32),
        VMEM((2, 3, TILE, POINTS * TILE), BF16),
        VMEM((2, 2, TILE, TILE), BF16),
    ]
    params = pltpu.CompilerParams(vmem_limit_bytes=12 << 20)
    sums = pl.pallas_call(
        functools.partial(own_kernel, half_tiles),
        out_shape=VMEM((row_tiles, bands, TILE), F32),
        in_specs=[smem] * 4 + [whole()] * 5 + [whole(pltpu.HBM)],
        out_specs=whole(),
        scratch_shapes=[
            VMEM(static_tiles.shape[2:], static_tiles.dtype),
            pltpu.SemaphoreType.DMA,
        ]
        + scratch,
        compiler_params=params,
        name="own",
    )(
        lists, counts, static_list, spots, left, centre, visibility[0, 0], rad, keep,
        in_hbm(static_tiles[0, 0]),
    )
    shape = jax.ShapeDtypeStruct((bands, patches), F32)
    mine, sent = pl.pallas_call(
        functools.partial(other_kernel, half_tiles, row_tiles // 2),
        out_shape=(shape, shape),
        in_specs=[smem] * 3 + [whole()] * 7,
        out_specs=(whole(), whole()),
        scratch_shapes=[VMEM((row_tiles, bands, TILE), F32)] + scratch,
        compiler_params=params,
        name="other",
    )(lists, counts, spots, left, centre, visibility[0, 0], rad, keep, other, sums)
    arrived = lax.ppermute(sent, "cols", [(0, 1), (1, 0)])
    return emission + albedo * (mine + arrived)


def solution(mesh):
    in_specs = (
        P(None, ("groups", "rows", "cols")),
        P(None, ("groups", "rows", "cols")),
        P(("groups", "rows", "cols")),
        P(),
        P(("groups", "rows"), "cols", None, None, None),
        P(("groups", "rows"), "cols", None, None),
        P(None, None, ("groups", "rows")),
        P(("groups", "cols"), "rows", None, None, None),
        P(("groups", "cols")),
        P(("groups", "rows"), None, None, None),
        P(("groups", "rows"), None),
        P(("groups", "rows"), "cols", None, None, None),
    )
    out_specs = P(None, ("groups", "rows", "cols"))
    return jax.shard_map(body, mesh=mesh, in_specs=in_specs, out_specs=out_specs, check_vma=False)
```

```python
import functools
import math

import jax
import jax.numpy as jnp
from jax import lax
from jax.experimental import pallas as pl
from jax.experimental.pallas import tpu as pltpu
from jax.sharding import PartitionSpec as P

TILE = 128
POINTS = 4
POS = 2.0**13
MOM = 2.0**19
RAD = 2.0**11
BATCH = 16
REFS = 8
GROUP = 16 * 12
F32 = jnp.float32
BF16 = jnp.bfloat16
VMEM = pltpu.VMEM
NT = (((1,), (1,)), ((), ()))


def hop_orders(rows):
    high = [rows >> shift for shift in range(1, rows.bit_length() - 1)]
    return [1] + high, high + [1]


def bit_of(level, rows):
    first, second = hop_orders(rows)
    return jnp.where(lax.axis_index("cols") == 0, first[level], second[level])


def held_half():
    return ((lax.axis_index("rows") & bit_of(0, lax.axis_size("rows"))) != 0).astype(jnp.int32)


def whole(memory_space=VMEM):
    return pl.BlockSpec(memory_space=memory_space)


def in_hbm(value):
    return pltpu.with_memory_space_constraint(value, pltpu.HBM)


def parts3(value):
    first = value.astype(BF16)
    rest = value - first.astype(F32)
    second = rest.astype(BF16)
    third = (rest - second.astype(F32)).astype(BF16)
    return first, second, third


def encode_points(half_tiles, half, geo_hbm, geo_ref, arrived, out_ref):
    lanes = half_tiles * TILE
    part = pl.ds(pl.multiple_of(half * lanes, TILE), lanes)
    fields = [
        pltpu.make_async_copy(geo_hbm.at[field, :, part], geo_ref.at[field], arrived.at[field])
        for field in range(6)
    ]
    for field in (3, 4, 5, 0, 1, 2):
        fields[field].start()
    for field in (3, 4, 5):
        fields[field].wait()
    angles = jnp.concatenate([geo_ref[3], geo_ref[4]], axis=0)
    sines, cosines = jnp.sin(angles), jnp.cos(angles)
    area = geo_ref[5]
    normal = (
        sines[0:4] * cosines[4:8],
        sines[0:4] * sines[4:8],
        cosines[0:4],
    )
    point_rows = 12 * half_tiles
    for axis in range(3):
        fields[axis].wait()
        place = geo_ref[axis]
        centre = jnp.floor(place[0:1, 0:1] + 0.5)
        moved = jnp.floor((place - centre) * POS + 0.5).astype(jnp.int32)
        moved = jnp.clip(moved, -32768, 32767)
        moment = jnp.floor(area * normal[axis] * MOM + 0.5).astype(jnp.int32)
        moment = jnp.clip(moment, -32768, 32767)
        words = (moved << 16) | (moment & 65535)
        for tile in range(half_tiles):
            row = 12 * tile + 4 * axis
            out_ref[row : row + 4, :] = words[:, tile * TILE : (tile + 1) * TILE]
        row = point_rows + axis
        out_ref[row : row + 1, :] = jnp.broadcast_to(centre.astype(jnp.int32), (1, TILE))
    out_ref[point_rows + 3 : point_rows + REFS, :] = jnp.zeros((REFS - 3, TILE), jnp.int32)


def send_kernel(half_tiles, geo_hbm, rad_hbm, send_ref, words_ref, geo_ref, rad_ref, arrived):
    own_rad = pltpu.make_async_copy(rad_hbm, rad_ref, arrived.at[6])
    own_rad.start()
    encode_points(half_tiles, 1 - held_half(), geo_hbm, geo_ref, arrived, send_ref)
    own_rad.wait()
    rad = (rad_ref[...].astype(F32) * RAD).astype(jnp.int32)
    rad = (rad[0:2] << 16) | rad[2:4]
    for tile in range(rad.shape[1] // TILE):
        words_ref[2 * tile : 2 * tile + 2, :] = rad[:, tile * TILE : (tile + 1) * TILE]
    send_ref[12 * half_tiles + REFS :, :] = words_ref[...]


def keep_kernel(half_tiles, geo_hbm, row_hbm, keep_ref, row_ref, geo_ref, arrived):
    rows = pltpu.make_async_copy(row_hbm, row_ref, arrived.at[6])
    rows.start()
    encode_points(half_tiles, held_half(), geo_hbm, geo_ref, arrived, keep_ref)
    rows.wait()


def rows_kernel(low, high, list_ref, count_ref, geo_ref, after, *refs):
    left_ref, centre_ref, columns = refs[-3:]
    group = lax.axis_index("cols")
    columns[...] = jnp.zeros_like(columns)
    lane_row = lax.broadcasted_iota(jnp.int32, (8, TILE), 0)
    ones = jnp.where(lane_row < 3, 1.0, 0.0).astype(F32)
    blank = jnp.zeros((8, TILE), F32)
    centre_ref[...] = blank
    centre = []
    for axis in range(3):
        first = jnp.floor(geo_ref[axis, 0:1, 0:1] + 0.5)
        centre.append(first)
        centre_ref[axis : axis + 1, :] = jnp.broadcast_to(first, (1, TILE))

    def one_slot(slot, carry):
        start = pl.multiple_of(list_ref[group, 0, slot] * TILE, TILE)
        slab = [geo_ref[field, :, pl.ds(start, TILE)] for field in range(5)]
        place = [slab[axis] - centre[axis] for axis in range(3)]
        angles = jnp.concatenate([slab[3], slab[4]], axis=0)
        sines, cosines = jnp.sin(angles), jnp.cos(angles)
        normal = (sines[0:4] * cosines[4:8], sines[0:4] * sines[4:8], cosines[0:4])
        shift = -(normal[0] * place[0] + normal[1] * place[1] + normal[2] * place[2])
        square = place[0] * place[0] + place[1] * place[1] + place[2] * place[2]

        def put(row, value):
            columns[pl.ds(row, POINTS, stride=64), :] = value.astype(F32)

        for axis in range(3):
            for part, value in enumerate(parts3(normal[axis])):
                put(8 * part + axis, value)
            for part, value in enumerate(parts3(place[axis])):
                put(32 + 8 * part + axis, value)
        for part, value in enumerate(parts3(shift)):
            put(24 + part, value)
        for part, value in enumerate(parts3(square)):
            put(56 + part, value)
        for point in range(POINTS):
            block = [columns[64 * point + 8 * i : 64 * point + 8 * i + 8, :] for i in range(8)]
            n1, n2, n3, c, x1, x2, x3, q = block
            both = [n1, n1, n1, n2, n2, n3, c, blank, q, x1, x1, x1, x2, x2, x3, ones]
            at = pl.ds(point * TILE, TILE)
            left_ref[slot, at, :] = jnp.concatenate(both, axis=0).astype(BF16).T
        return carry

    lax.fori_loop(low, jnp.minimum(count_ref[group], high), one_slot, 0)


def radiosity_of(rad_ref, spot):
    pair = rad_ref[pl.ds(2 * spot, 2), :]
    both = jnp.concatenate([pair >> 16, pair & 65535], axis=0)
    return (both.astype(F32) * (1.0 / RAD)).astype(BF16)


def slots_of_half(
    half_tiles, last_half, list_ref, count_ref, spot_ref, left_ref, centre_ref, visible_ref, rad_ref,
    points, total, words, away, order, right, gains,
):
    group = lax.axis_index("cols")
    held = held_half()
    point_rows = 12 * half_tiles
    sub = lax.broadcasted_iota(jnp.int32, (8, POINTS * TILE), 0)
    valid = sub < 3
    for half, points_ref in enumerate(points):
        words[half, 0 : point_rows + REFS, :] = points_ref[...]
        apart = points_ref[point_rows:, :].astype(F32) - centre_ref[...]
        away[half] = jnp.concatenate([apart] * POINTS, axis=1)
    blank = jnp.zeros((8, POINTS * TILE), F32)
    ones = jnp.where(valid, 1.0, 0.0).astype(F32)

    def half_of(slot):
        return (list_ref[group, 1, slot] // half_tiles) ^ held

    def pick(slot, seen):
        found, odd = seen
        late = half_of(slot)
        order[jnp.where(late == int(last_half), found, order.shape[0] - 1)] = slot
        return found + (late == int(last_half)).astype(jnp.int32), jnp.where(late == 0, slot, odd)

    count = count_ref[group]
    found, latest = lax.fori_loop(0, count, pick, (jnp.int32(0), jnp.int32(0)))
    if last_half:
        spare = (count - found) % 2
        order[jnp.where(spare == 1, found, order.shape[0] - 1)] = latest
        found = found + spare
    else:
        found = found - found % 2

    def stack3(value):
        first, second, third = (part.astype(F32) for part in parts3(value))
        return jnp.where(sub == 0, first, jnp.where(sub == 1, second, jnp.where(valid, third, 0.0)))

    def split(value):
        return [part.astype(F32) for part in parts3(value)]

    def prepare(index, which):
        slot = order[index]
        half = half_of(slot) if last_half else 0
        start = (list_ref[group, 1, slot] % half_tiles) * 12
        word = jnp.concatenate(
            [words[half, pl.ds(start + point, 8, stride=POINTS), :] for point in range(POINTS)], axis=1
        )
        place = jnp.where(valid, (word >> 16).astype(F32) * (1.0 / POS) + away[half], 0.0)
        moment = jnp.where(valid, ((word << 16) >> 16).astype(F32) * (1.0 / MOM), 0.0)
        area = jnp.sqrt(jnp.sum(moment * moment, axis=0, keepdims=True))
        shift = stack3(-jnp.sum(moment * place, axis=0, keepdims=True))
        square = stack3(jnp.sum(place * place, axis=0, keepdims=True) + area)
        x1, x2, x3 = split(place)
        m1, m2, m3 = split(moment)
        y1, y2, y3 = -2.0 * x1, -2.0 * x2, -2.0 * x3
        empty = [blank] * 8
        right[which, 0] = jnp.concatenate([x1, x2, x3, x1, x2, x1, ones, blank] + empty, axis=0).astype(BF16)
        right[which, 1] = jnp.concatenate(empty + [blank, m1, m2, m3, m1, m2, m1, shift], axis=0).astype(BF16)
        right[which, 2] = jnp.concatenate(empty + [ones, y1, y2, y3, y1, y2, y1, square], axis=0).astype(BF16)

    def finish(index, which):
        slot = order[index]
        rad = radiosity_of(rad_ref, spot_ref[spot_ref.shape[0] - list_ref.shape[2] + slot])
        part = lax.dot_general(rad, gains[which, 0], NT, preferred_element_type=F32)
        part = part + lax.dot_general(rad, gains[which, 1], NT, preferred_element_type=F32)
        row = list_ref[group, 0, slot]
        total[row] = total[row] + part * (1.0 / (math.pi * POINTS))

    def make(index, which):
        slot = order[index]
        gain = None
        for pair in range(POINTS // 2):
            at = slice(2 * pair * TILE, 2 * (pair + 1) * TILE)
            left = left_ref[slot]
            facing = jnp.dot(left, right[which, 0, :, at], preferred_element_type=F32)
            toward = jnp.dot(left, right[which, 1, :, at], preferred_element_type=F32)
            spread = jnp.dot(left, right[which, 2, :, at], preferred_element_type=F32)
            over = jnp.maximum(facing, 0.0) * jnp.maximum(toward, 0.0)
            under = spread * spread
            over_a, over_b = over[:, :TILE], over[:, TILE:]
            under_a, under_b = under[:, :TILE], under[:, TILE:]
            term = (over_a * under_b + over_b * under_a) / (under_a * under_b)
            for point in range(POINTS):
                one = term[point * TILE : (point + 1) * TILE]
                gain = one if gain is None else gain + one
        return gain * visible_ref[slot].astype(F32)

    def keep(gain, which):
        high = gain.astype(BF16)
        gains[which, 0] = high
        gains[which, 1] = (gain - high.astype(F32)).astype(BF16)

    def two_slots(index, carry):
        first = 2 * index
        second = jnp.minimum(first + 1, found - 1)
        live = jnp.where(first + 1 < found, 1.0, 0.0)
        finish(jnp.maximum(first - 2, 0), 0)
        finish(jnp.maximum(first - 1, 0), 1)
        gain_a = make(first, 0)
        gain_b = make(second, 1) * live
        prepare(jnp.minimum(first + 2, found - 1), 0)
        prepare(jnp.minimum(first + 3, found - 1), 1)
        keep(gain_a, 0)
        keep(gain_b, 1)
        return carry

    @pl.when(found > 0)
    def _():
        gains[...] = jnp.zeros_like(gains)
        prepare(0, 0)
        prepare(jnp.minimum(1, found - 1), 1)
        trips = (found + 1) // 2
        lax.fori_loop(0, trips, two_slots, 0)
        finish(2 * trips - 2, 0)
        finish(jnp.minimum(2 * trips - 1, found - 1), 1)


def own_kernel(
    half_tiles, list_ref, count_ref, static_ref, spot_ref, left_ref, centre_ref,
    visible_ref, rad_ref, points_ref, tiles_hbm, total_ref, tiles, arrived, words, away, order, right, gains,
):
    copy = pltpu.make_async_copy(tiles_hbm, tiles, arrived)
    copy.start()
    total_ref[...] = jnp.zeros_like(total_ref)
    slots_of_half(
        half_tiles, False, list_ref, count_ref, spot_ref, left_ref, centre_ref,
        visible_ref, rad_ref, [points_ref], total_ref, words, away, order, right, gains,
    )
    copy.wait()
    for first in range(0, tiles.shape[0], BATCH):
        parts = []
        for one in range(first, first + BATCH):
            rad = radiosity_of(rad_ref, spot_ref[one])
            parts.append(lax.dot_general(rad, tiles[one], NT, preferred_element_type=F32))
        for step, part in enumerate(parts):
            row = static_ref[0, first + step]
            total_ref[row] = total_ref[row] + part


def other_kernel(
    half_tiles, out_tiles, list_ref, count_ref, spot_ref, left_ref, centre_ref, visible_ref, rad_ref,
    own_ref, points_ref, sum_ref, keep_ref, send_ref, total, words, away, order, right, gains,
):
    group = lax.axis_index("cols")
    total[...] = sum_ref[...]
    slots_of_half(
        half_tiles, True, list_ref, count_ref, spot_ref, left_ref, centre_ref,
        visible_ref, rad_ref, [own_ref, points_ref], total, words, away, order, right, gains,
    )
    for tile in range(out_tiles):
        at = slice(tile * TILE, (tile + 1) * TILE)
        keep_ref[:, at] = total[group * out_tiles + tile]
        send_ref[:, at] = total[(1 - group) * out_tiles + tile]


def body(
    radiosity,
    emission,
    material,
    reflectance,
    static_tiles,
    static_index,
    row_geometry,
    array_geometry,
    array_owner,
    array_index,
    array_count,
    visibility,
):
    rows = lax.axis_size("rows")
    me = lax.axis_index("rows")
    owner = array_owner[0]
    bands, patches = radiosity.shape
    own_tiles = patches // TILE
    row_tiles = row_geometry.shape[2] // TILE
    array_tiles = array_geometry.shape[-1] // TILE
    half_tiles = array_tiles // 2
    half_rows = 12 * half_tiles + REFS
    rad_rows = 2 * own_tiles
    slots = visibility.shape[2]
    column_tiles = own_tiles * rows

    levels = rows.bit_length() - 1
    orders = hop_orders(rows)

    def hop(value, level):
        pairs = [
            (2 * row + col, 2 * (row ^ orders[col][level]) + col) for row in range(rows) for col in range(2)
        ]
        return lax.ppermute(value, ("rows", "cols"), pairs)

    def better(mine, theirs, level):
        return jnp.where(((owner ^ me) & bit_of(level, rows)) != 0, theirs, mine)

    half_shape = (*array_geometry.shape[2:4], half_tiles * TILE)
    candidates = in_hbm(array_geometry[0, 0])
    hbm = whole(pltpu.HBM)
    small = pltpu.CompilerParams(vmem_limit_bytes=4 << 20)
    send, rad = pl.pallas_call(
        functools.partial(send_kernel, half_tiles),
        out_shape=(VMEM((half_rows + rad_rows, TILE), jnp.int32), VMEM((rad_rows, TILE), jnp.int32)),
        in_specs=[hbm, hbm],
        out_specs=(whole(), whole()),
        scratch_shapes=[
            VMEM(half_shape, F32),
            VMEM(radiosity.shape, radiosity.dtype),
            pltpu.SemaphoreType.DMA((7,)),
        ],
        compiler_params=small,
        name="send",
    )(candidates, in_hbm(radiosity))
    keep, geometry = pl.pallas_call(
        functools.partial(keep_kernel, half_tiles),
        out_shape=(VMEM((half_rows, TILE), jnp.int32), VMEM(row_geometry.shape, F32)),
        in_specs=[hbm, hbm],
        out_specs=(whole(), whole()),
        scratch_shapes=[VMEM(half_shape, F32), pltpu.SemaphoreType.DMA((7,))],
        compiler_params=small,
        name="keep",
    )(candidates, in_hbm(row_geometry))
    smem = whole(pltpu.SMEM)
    lists = array_index[0]
    counts = array_count[0]

    def rows_call(low, high, after, *so_far):
        return pl.pallas_call(
            functools.partial(rows_kernel, low, high),
            out_shape=(VMEM((slots, POINTS * TILE, TILE), BF16), VMEM((8, TILE), F32)),
            in_specs=[smem, smem, whole(), whole(pl.ANY)] + [whole()] * len(so_far),
            out_specs=(whole(), whole()),
            input_output_aliases={4: 0, 5: 1} if so_far else {},
            scratch_shapes=[VMEM((POINTS * 64, TILE), F32)],
            compiler_params=small,
            name="rows_low" if low == 0 else "rows_high",
        )(lists, counts, geometry, after, *so_far)

    for level in range(levels):
        got = hop(send, level)
        if level == 1:
            left, centre = rows_call(0, slots // 2, keep)
            got, left = lax.optimization_barrier((got, left))
        keep = better(keep, got[:half_rows], level)
        rad = jnp.concatenate([rad, got[half_rows:]], axis=0)
        send = jnp.concatenate([keep, rad], axis=0)
        if level == 1:
            left, centre = rows_call(slots // 2, slots, keep, left, centre)
    other = hop(keep, 0)

    def spot(column_tile):
        holder = (column_tile // own_tiles) ^ me
        place = jnp.zeros_like(column_tile)
        for level in range(levels):
            place = place + jnp.where((holder & bit_of(level, rows)) != 0, 1 << level, 0)
        return place * own_tiles + column_tile % own_tiles

    group = lax.axis_index("cols")
    static_list = static_index[0, 0]
    spots = spot(jnp.concatenate([static_list[1], column_tiles - array_tiles + lists[group, 1]]))
    onehot = (jnp.arange(reflectance.shape[1], dtype=jnp.int32)[:, None] == material[None, :]).astype(F32)
    albedo = jnp.dot(reflectance, onehot, precision=lax.Precision.HIGHEST)

    scratch = [
        VMEM((2, half_rows + 16, TILE), jnp.int32),
        VMEM((2, 8, POINTS * TILE), F32),
        pltpu.SMEM((slots + 1,), jnp.int32),
        VMEM((2, 3, TILE, POINTS * TILE), BF16),
        VMEM((2, 2, TILE, TILE), BF16),
    ]
    params = pltpu.CompilerParams(vmem_limit_bytes=12 << 20)
    sums = pl.pallas_call(
        functools.partial(own_kernel, half_tiles),
        out_shape=VMEM((row_tiles, bands, TILE), F32),
        in_specs=[smem] * 4 + [whole()] * 5 + [whole(pltpu.HBM)],
        out_specs=whole(),
        scratch_shapes=[
            VMEM(static_tiles.shape[2:], static_tiles.dtype),
            pltpu.SemaphoreType.DMA,
        ]
        + scratch,
        compiler_params=params,
        name="own",
    )(
        lists, counts, static_list, spots, left, centre, visibility[0, 0], rad, keep,
        in_hbm(static_tiles[0, 0]),
    )
    shape = jax.ShapeDtypeStruct((bands, patches), F32)
    mine, sent = pl.pallas_call(
        functools.partial(other_kernel, half_tiles, row_tiles // 2),
        out_shape=(shape, shape),
        in_specs=[smem] * 3 + [whole()] * 7,
        out_specs=(whole(), whole()),
        scratch_shapes=[VMEM((row_tiles, bands, TILE), F32)] + scratch,
        compiler_params=params,
        name="other",
    )(lists, counts, spots, left, centre, visibility[0, 0], rad, keep, other, sums)
    arrived = lax.ppermute(sent, "cols", [(0, 1), (1, 0)])
    return emission + albedo * (mine + arrived)


def solution(mesh):
    in_specs = (
        P(None, ("groups", "rows", "cols")),
        P(None, ("groups", "rows", "cols")),
        P(("groups", "rows", "cols")),
        P(),
        P(("groups", "rows"), "cols", None, None, None),
        P(("groups", "rows"), "cols", None, None),
        P(None, None, ("groups", "rows")),
        P(("groups", "cols"), "rows", None, None, None),
        P(("groups", "cols")),
        P(("groups", "rows"), None, None, None),
        P(("groups", "rows"), None),
        P(("groups", "rows"), "cols", None, None, None),
    )
    out_specs = P(None, ("groups", "rows", "cols"))
    return jax.shard_map(body, mesh=mesh, in_specs=in_specs, out_specs=out_specs, check_vma=False)
```

```python
import functools
import math

import jax
import jax.numpy as jnp
from jax import lax
from jax.experimental import pallas as pl
from jax.experimental.pallas import tpu as pltpu
from jax.sharding import PartitionSpec as P

TILE = 128
POINTS = 4
POS = 2.0**13
MOM = 2.0**19
RAD = 2.0**11
BATCH = 16
PLACES = 64
REFS = 8
GROUP = 16 * 12
F32 = jnp.float32
BF16 = jnp.bfloat16
VMEM = pltpu.VMEM
NT = (((1,), (1,)), ((), ()))


def hop_orders(rows):
    high = [rows >> shift for shift in range(1, rows.bit_length() - 1)]
    return [1] + high, high + [1]


def bit_of(level, rows):
    first, second = hop_orders(rows)
    return jnp.where(lax.axis_index("cols") == 0, first[level], second[level])


def held_half():
    return ((lax.axis_index("rows") & bit_of(0, lax.axis_size("rows"))) != 0).astype(jnp.int32)


def whole(memory_space=VMEM):
    return pl.BlockSpec(memory_space=memory_space)


def in_hbm(value):
    return pltpu.with_memory_space_constraint(value, pltpu.HBM)


def parts3(value):
    first = value.astype(BF16)
    rest = value - first.astype(F32)
    second = rest.astype(BF16)
    third = (rest - second.astype(F32)).astype(BF16)
    return first, second, third


def encode_points(half_tiles, half, geo_hbm, geo_ref, arrived, out_ref):
    lanes = half_tiles * TILE
    part = pl.ds(pl.multiple_of(half * lanes, TILE), lanes)
    fields = [
        pltpu.make_async_copy(geo_hbm.at[field, :, part], geo_ref.at[field], arrived.at[field])
        for field in range(6)
    ]
    for field in (3, 4, 5, 0, 1, 2):
        fields[field].start()
    for field in (3, 4, 5):
        fields[field].wait()
    angles = jnp.concatenate([geo_ref[3], geo_ref[4]], axis=0)
    sines, cosines = jnp.sin(angles), jnp.cos(angles)
    area = geo_ref[5]
    normal = (
        sines[0:4] * cosines[4:8],
        sines[0:4] * sines[4:8],
        cosines[0:4],
    )
    point_rows = 12 * half_tiles
    for axis in range(3):
        fields[axis].wait()
        place = geo_ref[axis]
        centre = jnp.floor(place[0:1, 0:1] + 0.5)
        moved = jnp.floor((place - centre) * POS + 0.5).astype(jnp.int32)
        moved = jnp.clip(moved, -32768, 32767)
        moment = jnp.floor(area * normal[axis] * MOM + 0.5).astype(jnp.int32)
        moment = jnp.clip(moment, -32768, 32767)
        words = (moved << 16) | (moment & 65535)
        for tile in range(half_tiles):
            row = 12 * tile + 4 * axis
            out_ref[row : row + 4, :] = words[:, tile * TILE : (tile + 1) * TILE]
        row = point_rows + axis
        out_ref[row : row + 1, :] = jnp.broadcast_to(centre.astype(jnp.int32), (1, TILE))
    out_ref[point_rows + 3 : point_rows + REFS, :] = jnp.zeros((REFS - 3, TILE), jnp.int32)


def send_kernel(half_tiles, geo_hbm, rad_hbm, send_ref, words_ref, geo_ref, rad_ref, arrived):
    own_rad = pltpu.make_async_copy(rad_hbm, rad_ref, arrived.at[6])
    own_rad.start()
    encode_points(half_tiles, 1 - held_half(), geo_hbm, geo_ref, arrived, send_ref)
    own_rad.wait()
    rad = (rad_ref[...].astype(F32) * RAD).astype(jnp.int32)
    rad = (rad[0:2] << 16) | rad[2:4]
    for tile in range(rad.shape[1] // TILE):
        words_ref[2 * tile : 2 * tile + 2, :] = rad[:, tile * TILE : (tile + 1) * TILE]
    send_ref[12 * half_tiles + REFS :, :] = words_ref[...]


def keep_kernel(half_tiles, geo_hbm, row_hbm, keep_ref, row_ref, geo_ref, arrived):
    rows = pltpu.make_async_copy(row_hbm, row_ref, arrived.at[6])
    rows.start()
    encode_points(half_tiles, held_half(), geo_hbm, geo_ref, arrived, keep_ref)
    rows.wait()


def make_plan(half_tiles, list_ref, count_ref, plan_ref):
    group = lax.axis_index("cols")
    held = held_half()
    dummy = plan_ref.shape[1] - 1

    def pick(slot, seen):
        late = (list_ref[group, 1, slot] // half_tiles) ^ held
        plan_ref[0, jnp.where(late == 0, seen[0], dummy)] = slot
        plan_ref[1, jnp.where(late == 1, seen[1], dummy)] = slot
        return seen[0] + 1 - late, seen[1] + late

    first, found = lax.fori_loop(0, count_ref[group], pick, (jnp.int32(0), jnp.int32(0)))
    spare = first % 2
    plan_ref[1, jnp.where(spare == 1, found, dummy)] = plan_ref[0, jnp.maximum(first - 1, 0)]
    plan_ref[2, 0] = first - spare
    plan_ref[2, 1] = found + spare


def rows_kernel(low, high, half_tiles, list_ref, count_ref, geo_ref, after, *refs):
    if low == 0:
        left_ref, centre_ref, plan_ref, columns = refs
        make_plan(half_tiles, list_ref, count_ref, plan_ref)
    else:
        left_ref, centre_ref, columns = refs[-3:]
    group = lax.axis_index("cols")
    columns[...] = jnp.zeros_like(columns)
    lane_row = lax.broadcasted_iota(jnp.int32, (8, TILE), 0)
    ones = jnp.where(lane_row < 3, 1.0, 0.0).astype(F32)
    blank = jnp.zeros((8, TILE), F32)
    centre_ref[...] = blank
    centre = []
    for axis in range(3):
        first = jnp.floor(geo_ref[axis, 0:1, 0:1] + 0.5)
        centre.append(first)
        centre_ref[axis : axis + 1, :] = jnp.broadcast_to(first, (1, TILE))

    def one_slot(slot, carry):
        start = pl.multiple_of(list_ref[group, 0, slot] * TILE, TILE)
        slab = [geo_ref[field, :, pl.ds(start, TILE)] for field in range(5)]
        place = [slab[axis] - centre[axis] for axis in range(3)]
        angles = jnp.concatenate([slab[3], slab[4]], axis=0)
        sines, cosines = jnp.sin(angles), jnp.cos(angles)
        normal = (sines[0:4] * cosines[4:8], sines[0:4] * sines[4:8], cosines[0:4])
        shift = -(normal[0] * place[0] + normal[1] * place[1] + normal[2] * place[2])
        square = place[0] * place[0] + place[1] * place[1] + place[2] * place[2]

        def put(row, value):
            columns[pl.ds(row, POINTS, stride=64), :] = value.astype(F32)

        for axis in range(3):
            for part, value in enumerate(parts3(normal[axis])):
                put(8 * part + axis, value)
            for part, value in enumerate(parts3(place[axis])):
                put(32 + 8 * part + axis, value)
        for part, value in enumerate(parts3(shift)):
            put(24 + part, value)
        for part, value in enumerate(parts3(square)):
            put(56 + part, value)
        for point in range(POINTS):
            block = [columns[64 * point + 8 * i : 64 * point + 8 * i + 8, :] for i in range(8)]
            n1, n2, n3, c, x1, x2, x3, q = block
            both = [q, x1, x1, x1, x2, x2, x3, ones, n1, n1, n1, n2, n2, n3, c, blank]
            at = pl.ds(point * TILE, TILE)
            left_ref[slot, at, :] = jnp.concatenate(both, axis=0).astype(BF16).T
        return carry

    lax.fori_loop(low, jnp.minimum(count_ref[group], high), one_slot, 0)


def radiosity_of(rad_ref, spot):
    pair = rad_ref[pl.ds(2 * spot, 2), :]
    both = jnp.concatenate([pair >> 16, pair & 65535], axis=0)
    return (both.astype(F32) * (1.0 / RAD)).astype(BF16)


def slots_of_half(
    half_tiles, last_half, list_ref, plan_ref, spot_ref, left_ref, centre_ref, visible_ref, rad_ref,
    points, total, words, away, right, gains,
):
    group = lax.axis_index("cols")
    held = held_half()
    point_rows = 12 * half_tiles
    sub = lax.broadcasted_iota(jnp.int32, (8, POINTS * TILE), 0)
    valid = sub < 3
    for half, points_ref in enumerate(points):
        words[half, 0 : point_rows + REFS, :] = points_ref[...]
        apart = points_ref[point_rows:, :].astype(F32) - centre_ref[...]
        away[half] = jnp.concatenate([apart] * POINTS, axis=1)
    blank = jnp.zeros((8, POINTS * TILE), F32)
    ones = jnp.where(valid, 1.0, 0.0).astype(F32)

    def half_of(slot):
        return (list_ref[group, 1, slot] // half_tiles) ^ held

    this = int(last_half)
    found = plan_ref[2, this]

    def stack3(value):
        first, second, third = (part.astype(F32) for part in parts3(value))
        return jnp.where(sub == 0, first, jnp.where(sub == 1, second, jnp.where(valid, third, 0.0)))

    def split(value):
        return [part.astype(F32) for part in parts3(value)]

    def prepare(index, which):
        slot = plan_ref[this, index]
        half = half_of(slot) if last_half else 0
        start = (list_ref[group, 1, slot] % half_tiles) * 12
        word = jnp.concatenate(
            [words[half, pl.ds(start + point, 8, stride=POINTS), :] for point in range(POINTS)], axis=1
        )
        place = jnp.where(valid, (word >> 16).astype(F32) * (1.0 / POS) + away[half], 0.0)
        moment = jnp.where(valid, ((word << 16) >> 16).astype(F32) * (1.0 / MOM), 0.0)
        area = jnp.sqrt(jnp.sum(moment * moment, axis=0, keepdims=True))
        shift = stack3(-jnp.sum(moment * place, axis=0, keepdims=True))
        square = stack3(jnp.sum(place * place, axis=0, keepdims=True) + area)
        x1, x2, x3 = split(place)
        m1, m2, m3 = split(moment)
        y1, y2, y3 = -2.0 * x1, -2.0 * x2, -2.0 * x3
        right_f = [blank] * 8 + [x1, x2, x3, x1, x2, x1, ones, blank]
        right[which, 0] = jnp.concatenate(right_f, axis=0).astype(BF16)
        right_t = jnp.concatenate([blank, m1, m2, m3, m1, m2, m1, shift], axis=0)
        right[which, 1, 0:PLACES] = right_t.astype(BF16)
        right_s = jnp.concatenate([ones, y1, y2, y3, y1, y2, y1, square], axis=0)
        right[which, 2, 0:PLACES] = right_s.astype(BF16)

    def finish(index, which):
        slot = plan_ref[this, index]
        rad = radiosity_of(rad_ref, spot_ref[spot_ref.shape[0] - list_ref.shape[2] + slot])
        part = lax.dot_general(rad, gains[which, 0], NT, preferred_element_type=F32)
        part = part + lax.dot_general(rad, gains[which, 1], NT, preferred_element_type=F32)
        row = list_ref[group, 0, slot]
        total[row] = total[row] + part * (1.0 / (math.pi * POINTS))

    def make(index, which):
        slot = plan_ref[this, index]
        gain = None
        for pair in range(POINTS // 2):
            at = slice(2 * pair * TILE, 2 * (pair + 1) * TILE)
            left = left_ref[slot]
            facing = jnp.dot(left, right[which, 0, :, at], preferred_element_type=F32)
            near = left_ref[slot, :, 0:PLACES]
            toward = jnp.dot(near, right[which, 1, 0:PLACES, at], preferred_element_type=F32)
            spread = jnp.dot(near, right[which, 2, 0:PLACES, at], preferred_element_type=F32)
            over = jnp.maximum(facing, 0.0) * jnp.maximum(toward, 0.0)
            under = spread * spread
            over_a, over_b = over[:, :TILE], over[:, TILE:]
            under_a, under_b = under[:, :TILE], under[:, TILE:]
            term = (over_a * under_b + over_b * under_a) / (under_a * under_b)
            for point in range(POINTS):
                one = term[point * TILE : (point + 1) * TILE]
                gain = one if gain is None else gain + one
        return gain * visible_ref[slot].astype(F32)

    def keep(gain, which):
        high = gain.astype(BF16)
        gains[which, 0] = high
        gains[which, 1] = (gain - high.astype(F32)).astype(BF16)

    def two_slots(index, carry):
        first = 2 * index
        second = jnp.minimum(first + 1, found - 1)
        live = jnp.where(first + 1 < found, 1.0, 0.0)
        finish(jnp.maximum(first - 2, 0), 0)
        finish(jnp.maximum(first - 1, 0), 1)
        gain_a = make(first, 0)
        gain_b = make(second, 1) * live
        prepare(jnp.minimum(first + 2, found - 1), 0)
        prepare(jnp.minimum(first + 3, found - 1), 1)
        keep(gain_a, 0)
        keep(gain_b, 1)
        return carry

    @pl.when(found > 0)
    def _():
        gains[...] = jnp.zeros_like(gains)
        prepare(0, 0)
        prepare(jnp.minimum(1, found - 1), 1)
        trips = (found + 1) // 2
        lax.fori_loop(0, trips, two_slots, 0)
        finish(2 * trips - 2, 0)
        finish(jnp.minimum(2 * trips - 1, found - 1), 1)


def own_kernel(
    half_tiles, list_ref, plan_ref, static_ref, spot_ref, left_ref, centre_ref,
    visible_ref, rad_ref, points_ref, tiles_hbm, total_ref, tiles, arrived, words, away, right, gains,
):
    copy = pltpu.make_async_copy(tiles_hbm, tiles, arrived)
    copy.start()
    total_ref[...] = jnp.zeros_like(total_ref)
    slots_of_half(
        half_tiles, False, list_ref, plan_ref, spot_ref, left_ref, centre_ref,
        visible_ref, rad_ref, [points_ref], total_ref, words, away, right, gains,
    )
    copy.wait()
    for first in range(0, tiles.shape[0], BATCH):
        parts = []
        for one in range(first, first + BATCH):
            rad = radiosity_of(rad_ref, spot_ref[one])
            parts.append(lax.dot_general(rad, tiles[one], NT, preferred_element_type=F32))
        for step, part in enumerate(parts):
            row = static_ref[0, first + step]
            total_ref[row] = total_ref[row] + part


def other_kernel(
    half_tiles, out_tiles, list_ref, plan_ref, spot_ref, left_ref, centre_ref, visible_ref, rad_ref,
    own_ref, points_ref, sum_ref, keep_ref, send_ref, total, words, away, right, gains,
):
    group = lax.axis_index("cols")
    total[...] = sum_ref[...]
    slots_of_half(
        half_tiles, True, list_ref, plan_ref, spot_ref, left_ref, centre_ref,
        visible_ref, rad_ref, [own_ref, points_ref], total, words, away, right, gains,
    )
    for tile in range(out_tiles):
        at = slice(tile * TILE, (tile + 1) * TILE)
        keep_ref[:, at] = total[group * out_tiles + tile]
        send_ref[:, at] = total[(1 - group) * out_tiles + tile]


def body(
    radiosity,
    emission,
    material,
    reflectance,
    static_tiles,
    static_index,
    row_geometry,
    array_geometry,
    array_owner,
    array_index,
    array_count,
    visibility,
):
    rows = lax.axis_size("rows")
    me = lax.axis_index("rows")
    owner = array_owner[0]
    bands, patches = radiosity.shape
    own_tiles = patches // TILE
    row_tiles = row_geometry.shape[2] // TILE
    array_tiles = array_geometry.shape[-1] // TILE
    half_tiles = array_tiles // 2
    half_rows = 12 * half_tiles + REFS
    rad_rows = 2 * own_tiles
    slots = visibility.shape[2]
    column_tiles = own_tiles * rows

    levels = rows.bit_length() - 1
    orders = hop_orders(rows)

    def hop(value, level):
        pairs = [
            (2 * row + col, 2 * (row ^ orders[col][level]) + col) for row in range(rows) for col in range(2)
        ]
        return lax.ppermute(value, ("rows", "cols"), pairs)

    def better(mine, theirs, level):
        return jnp.where(((owner ^ me) & bit_of(level, rows)) != 0, theirs, mine)

    half_shape = (*array_geometry.shape[2:4], half_tiles * TILE)
    candidates = in_hbm(array_geometry[0, 0])
    hbm = whole(pltpu.HBM)
    small = pltpu.CompilerParams(vmem_limit_bytes=4 << 20)
    send, rad = pl.pallas_call(
        functools.partial(send_kernel, half_tiles),
        out_shape=(VMEM((half_rows + rad_rows, TILE), jnp.int32), VMEM((rad_rows, TILE), jnp.int32)),
        in_specs=[hbm, hbm],
        out_specs=(whole(), whole()),
        scratch_shapes=[
            VMEM(half_shape, F32),
            VMEM(radiosity.shape, radiosity.dtype),
            pltpu.SemaphoreType.DMA((7,)),
        ],
        compiler_params=small,
        name="send",
    )(candidates, in_hbm(radiosity))
    keep, geometry = pl.pallas_call(
        functools.partial(keep_kernel, half_tiles),
        out_shape=(VMEM((half_rows, TILE), jnp.int32), VMEM(row_geometry.shape, F32)),
        in_specs=[hbm, hbm],
        out_specs=(whole(), whole()),
        scratch_shapes=[VMEM(half_shape, F32), pltpu.SemaphoreType.DMA((7,))],
        compiler_params=small,
        name="keep",
    )(candidates, in_hbm(row_geometry))
    smem = whole(pltpu.SMEM)
    lists = array_index[0]
    counts = array_count[0]

    def rows_call(low, high, after, *so_far):
        out_shape = [VMEM((slots, POINTS * TILE, TILE), BF16), VMEM((8, TILE), F32)]
        out_specs = [whole(), whole()]
        if not so_far:
            out_shape.append(jax.ShapeDtypeStruct((3, slots + 1), jnp.int32))
            out_specs.append(smem)
        return pl.pallas_call(
            functools.partial(rows_kernel, low, high, half_tiles),
            out_shape=out_shape,
            in_specs=[smem, smem, whole(), whole(pl.ANY)] + [whole()] * len(so_far),
            out_specs=out_specs,
            input_output_aliases={4: 0, 5: 1} if so_far else {},
            scratch_shapes=[VMEM((POINTS * 64, TILE), F32)],
            compiler_params=small,
            name="rows_high" if so_far else "rows_low",
        )(lists, counts, geometry, after, *so_far)

    for level in range(levels):
        got = hop(send, level)
        if level == 1:
            left, centre, plan = rows_call(0, slots // 2, keep)
            got, left = lax.optimization_barrier((got, left))
        keep = better(keep, got[:half_rows], level)
        rad = jnp.concatenate([rad, got[half_rows:]], axis=0)
        send = jnp.concatenate([keep, rad], axis=0)
        if level == 1:
            left, centre = rows_call(slots // 2, slots, keep, left, centre)
    other = hop(keep, 0)

    def spot(column_tile):
        holder = (column_tile // own_tiles) ^ me
        place = jnp.zeros_like(column_tile)
        for level in range(levels):
            place = place + jnp.where((holder & bit_of(level, rows)) != 0, 1 << level, 0)
        return place * own_tiles + column_tile % own_tiles

    group = lax.axis_index("cols")
    static_list = static_index[0, 0]
    spots = spot(jnp.concatenate([static_list[1], column_tiles - array_tiles + lists[group, 1]]))
    onehot = (jnp.arange(reflectance.shape[1], dtype=jnp.int32)[:, None] == material[None, :]).astype(F32)
    albedo = jnp.dot(reflectance, onehot, precision=lax.Precision.HIGHEST)

    scratch = [
        VMEM((2, half_rows + 16, TILE), jnp.int32),
        VMEM((2, 8, POINTS * TILE), F32),
        VMEM((2, 3, TILE, POINTS * TILE), BF16),
        VMEM((2, 2, TILE, TILE), BF16),
    ]
    params = pltpu.CompilerParams(vmem_limit_bytes=12 << 20)
    sums = pl.pallas_call(
        functools.partial(own_kernel, half_tiles),
        out_shape=VMEM((row_tiles, bands, TILE), F32),
        in_specs=[smem] * 4 + [whole()] * 5 + [whole(pltpu.HBM)],
        out_specs=whole(),
        scratch_shapes=[
            VMEM(static_tiles.shape[2:], static_tiles.dtype),
            pltpu.SemaphoreType.DMA,
        ]
        + scratch,
        compiler_params=params,
        name="own",
    )(
        lists, plan, static_list, spots, left, centre, visibility[0, 0], rad, keep,
        in_hbm(static_tiles[0, 0]),
    )
    shape = jax.ShapeDtypeStruct((bands, patches), F32)
    mine, sent = pl.pallas_call(
        functools.partial(other_kernel, half_tiles, row_tiles // 2),
        out_shape=(shape, shape),
        in_specs=[smem] * 3 + [whole()] * 7,
        out_specs=(whole(), whole()),
        scratch_shapes=[VMEM((row_tiles, bands, TILE), F32)] + scratch,
        compiler_params=params,
        name="other",
    )(lists, plan, spots, left, centre, visibility[0, 0], rad, keep, other, sums)
    arrived = lax.ppermute(sent, "cols", [(0, 1), (1, 0)])
    return emission + albedo * (mine + arrived)


def solution(mesh):
    in_specs = (
        P(None, ("groups", "rows", "cols")),
        P(None, ("groups", "rows", "cols")),
        P(("groups", "rows", "cols")),
        P(),
        P(("groups", "rows"), "cols", None, None, None),
        P(("groups", "rows"), "cols", None, None),
        P(None, None, ("groups", "rows")),
        P(("groups", "cols"), "rows", None, None, None),
        P(("groups", "cols")),
        P(("groups", "rows"), None, None, None),
        P(("groups", "rows"), None),
        P(("groups", "rows"), "cols", None, None, None),
    )
    out_specs = P(None, ("groups", "rows", "cols"))
    return jax.shard_map(body, mesh=mesh, in_specs=in_specs, out_specs=out_specs, check_vma=False)
```

```python
import functools
import math

import jax
import jax.numpy as jnp
from jax import lax
from jax.experimental import pallas as pl
from jax.experimental.pallas import tpu as pltpu
from jax.sharding import PartitionSpec as P

TILE = 128
POINTS = 4
POS = 2.0**13
MOM = 2.0**19
RAD = 2.0**11
BATCH = 16
PLACES = 64
REFS = 8
GROUP = 16 * 12
F32 = jnp.float32
BF16 = jnp.bfloat16
VMEM = pltpu.VMEM
NT = (((1,), (1,)), ((), ()))


def hop_orders(rows):
    high = [rows >> shift for shift in range(1, rows.bit_length() - 1)]
    return [1] + high, high + [1]


def bit_of(level, rows):
    first, second = hop_orders(rows)
    return jnp.where(lax.axis_index("cols") == 0, first[level], second[level])


def held_half():
    return ((lax.axis_index("rows") & bit_of(0, lax.axis_size("rows"))) != 0).astype(jnp.int32)


def whole(memory_space=VMEM):
    return pl.BlockSpec(memory_space=memory_space)


def in_hbm(value):
    return pltpu.with_memory_space_constraint(value, pltpu.HBM)


def parts3(value):
    first = value.astype(BF16)
    rest = value - first.astype(F32)
    second = rest.astype(BF16)
    third = (rest - second.astype(F32)).astype(BF16)
    return first, second, third


def encode_points(half_tiles, half, geo_hbm, geo_ref, arrived, out_ref):
    lanes = half_tiles * TILE
    part = pl.ds(pl.multiple_of(half * lanes, TILE), lanes)
    fields = [
        pltpu.make_async_copy(geo_hbm.at[field, :, part], geo_ref.at[field], arrived.at[field])
        for field in range(6)
    ]
    for field in (3, 4, 5, 0, 1, 2):
        fields[field].start()
    for field in (3, 4, 5):
        fields[field].wait()
    angles = jnp.concatenate([geo_ref[3], geo_ref[4]], axis=0)
    sines, cosines = jnp.sin(angles), jnp.cos(angles)
    area = geo_ref[5]
    normal = (
        sines[0:4] * cosines[4:8],
        sines[0:4] * sines[4:8],
        cosines[0:4],
    )
    point_rows = 12 * half_tiles
    for axis in range(3):
        fields[axis].wait()
        place = geo_ref[axis]
        centre = jnp.floor(place[0:1, 0:1] + 0.5)
        moved = jnp.floor((place - centre) * POS + 0.5).astype(jnp.int32)
        moved = jnp.clip(moved, -32768, 32767)
        moment = jnp.floor(area * normal[axis] * MOM + 0.5).astype(jnp.int32)
        moment = jnp.clip(moment, -32768, 32767)
        words = (moved << 16) | (moment & 65535)
        for tile in range(half_tiles):
            row = 12 * tile + 4 * axis
            out_ref[row : row + 4, :] = words[:, tile * TILE : (tile + 1) * TILE]
        row = point_rows + axis
        out_ref[row : row + 1, :] = jnp.broadcast_to(centre.astype(jnp.int32), (1, TILE))
    out_ref[point_rows + 3 : point_rows + REFS, :] = jnp.zeros((REFS - 3, TILE), jnp.int32)


def send_kernel(half_tiles, geo_hbm, rad_hbm, send_ref, words_ref, geo_ref, rad_ref, arrived):
    own_rad = pltpu.make_async_copy(rad_hbm, rad_ref, arrived.at[6])
    own_rad.start()
    encode_points(half_tiles, 1 - held_half(), geo_hbm, geo_ref, arrived, send_ref)
    own_rad.wait()
    rad = (rad_ref[...].astype(F32) * RAD).astype(jnp.int32)
    rad = (rad[0:2] << 16) | rad[2:4]
    for tile in range(rad.shape[1] // TILE):
        words_ref[2 * tile : 2 * tile + 2, :] = rad[:, tile * TILE : (tile + 1) * TILE]
    send_ref[12 * half_tiles + REFS :, :] = words_ref[...]


def keep_kernel(half_tiles, geo_hbm, row_hbm, keep_ref, row_ref, geo_ref, arrived):
    rows = pltpu.make_async_copy(row_hbm, row_ref, arrived.at[6])
    rows.start()
    encode_points(half_tiles, held_half(), geo_hbm, geo_ref, arrived, keep_ref)
    rows.wait()


def make_plan(half_tiles, list_ref, count_ref, plan_ref):
    group = lax.axis_index("cols")
    held = held_half()
    dummy = plan_ref.shape[1] - 1

    def pick(slot, seen):
        late = (list_ref[group, 1, slot] // half_tiles) ^ held
        plan_ref[0, jnp.where(late == 0, seen[0], dummy)] = slot
        plan_ref[1, jnp.where(late == 1, seen[1], dummy)] = slot
        return seen[0] + 1 - late, seen[1] + late

    first, found = lax.fori_loop(0, count_ref[group], pick, (jnp.int32(0), jnp.int32(0)))
    spare = first % 2
    plan_ref[1, jnp.where(spare == 1, found, dummy)] = plan_ref[0, jnp.maximum(first - 1, 0)]
    plan_ref[2, 0] = first - spare
    plan_ref[2, 1] = found + spare


def rows_kernel(low, high, half_tiles, list_ref, count_ref, geo_ref, after, *refs):
    if low == 0:
        left_ref, centre_ref, plan_ref, columns = refs
        make_plan(half_tiles, list_ref, count_ref, plan_ref)
    else:
        left_ref, centre_ref, columns = refs[-3:]
    group = lax.axis_index("cols")
    columns[...] = jnp.zeros_like(columns)
    lane_row = lax.broadcasted_iota(jnp.int32, (8, TILE), 0)
    ones = jnp.where(lane_row < 3, 1.0, 0.0).astype(F32)
    blank = jnp.zeros((8, TILE), F32)
    centre_ref[...] = blank
    centre = []
    for axis in range(3):
        first = jnp.floor(geo_ref[axis, 0:1, 0:1] + 0.5)
        centre.append(first)
        centre_ref[axis : axis + 1, :] = jnp.broadcast_to(first, (1, TILE))

    def one_slot(slot, carry):
        start = pl.multiple_of(list_ref[group, 0, slot] * TILE, TILE)
        slab = [geo_ref[field, :, pl.ds(start, TILE)] for field in range(5)]
        place = [slab[axis] - centre[axis] for axis in range(3)]
        angles = jnp.concatenate([slab[3], slab[4]], axis=0)
        sines, cosines = jnp.sin(angles), jnp.cos(angles)
        normal = (sines[0:4] * cosines[4:8], sines[0:4] * sines[4:8], cosines[0:4])
        shift = -(normal[0] * place[0] + normal[1] * place[1] + normal[2] * place[2])
        square = place[0] * place[0] + place[1] * place[1] + place[2] * place[2]

        def put(row, value):
            columns[pl.ds(row, POINTS, stride=64), :] = value.astype(F32)

        for axis in range(3):
            for part, value in enumerate(parts3(normal[axis])):
                put(8 * part + axis, value)
            for part, value in enumerate(parts3(place[axis])):
                put(32 + 8 * part + axis, value)
        for part, value in enumerate(parts3(shift)):
            put(24 + part, value)
        for part, value in enumerate(parts3(square)):
            put(56 + part, value)
        for point in range(POINTS):
            block = [columns[64 * point + 8 * i : 64 * point + 8 * i + 8, :] for i in range(8)]
            n1, n2, n3, c, x1, x2, x3, q = block
            both = [q, x1, x1, x1, x2, x2, x3, ones, n1, n1, n1, n2, n2, n3, c, blank]
            at = pl.ds(point * TILE, TILE)
            left_ref[slot, at, :] = jnp.concatenate(both, axis=0).astype(BF16).T
        return carry

    lax.fori_loop(low, jnp.minimum(count_ref[group], high), one_slot, 0)


def radiosity_of(rad_ref, spot):
    pair = rad_ref[pl.ds(2 * spot, 2), :]
    both = jnp.concatenate([pair >> 16, pair & 65535], axis=0)
    return (both.astype(F32) * (1.0 / RAD)).astype(BF16)


def slots_of_half(
    half_tiles, last_half, list_ref, plan_ref, spot_ref, left_ref, centre_ref, visible_ref, rad_ref,
    points, total, words, away, right, gains,
):
    group = lax.axis_index("cols")
    held = held_half()
    point_rows = 12 * half_tiles
    sub = lax.broadcasted_iota(jnp.int32, (8, POINTS * TILE), 0)
    valid = sub < 3
    for half, points_ref in enumerate(points):
        words[half, 0 : point_rows + REFS, :] = points_ref[...]
        apart = points_ref[point_rows:, :].astype(F32) - centre_ref[...]
        away[half] = jnp.concatenate([apart] * POINTS, axis=1)
    blank = jnp.zeros((8, POINTS * TILE), F32)
    ones = jnp.where(valid, 1.0, 0.0).astype(F32)

    def half_of(slot):
        return (list_ref[group, 1, slot] // half_tiles) ^ held

    this = int(last_half)
    found = plan_ref[2, this]

    def stack3(value):
        first, second, third = (part.astype(F32) for part in parts3(value))
        return jnp.where(sub == 0, first, jnp.where(sub == 1, second, jnp.where(valid, third, 0.0)))

    def split(value):
        return [part.astype(F32) for part in parts3(value)]

    def prepare(index, which):
        slot = plan_ref[this, index]
        half = half_of(slot) if last_half else 0
        start = (list_ref[group, 1, slot] % half_tiles) * 12
        word = jnp.concatenate(
            [words[half, pl.ds(start + point, 8, stride=POINTS), :] for point in range(POINTS)], axis=1
        )
        place = jnp.where(valid, (word >> 16).astype(F32) * (1.0 / POS) + away[half], 0.0)
        moment = jnp.where(valid, ((word << 16) >> 16).astype(F32) * (1.0 / MOM), 0.0)
        area = jnp.sqrt(jnp.sum(moment * moment, axis=0, keepdims=True))
        shift = stack3(-jnp.sum(moment * place, axis=0, keepdims=True))
        square = stack3(jnp.sum(place * place, axis=0, keepdims=True) + area)
        x1, x2, x3 = split(place)
        m1, m2, m3 = split(moment)
        y1, y2, y3 = -2.0 * x1, -2.0 * x2, -2.0 * x3
        right_f = [blank] * 8 + [x1, x2, x3, x1, x2, x1, ones, blank]
        right[which, 0] = jnp.concatenate(right_f, axis=0).astype(BF16)
        right_t = jnp.concatenate([blank, m1, m2, m3, m1, m2, m1, shift], axis=0)
        right[which, 1, 0:PLACES] = right_t.astype(BF16)
        right_s = jnp.concatenate([ones, y1, y2, y3, y1, y2, y1, square], axis=0)
        right[which, 2, 0:PLACES] = right_s.astype(BF16)

    def finish(index, which):
        slot = plan_ref[this, index]
        rad = radiosity_of(rad_ref, spot_ref[spot_ref.shape[0] - list_ref.shape[2] + slot])
        twice = jnp.concatenate([rad, rad], axis=1)
        part = lax.dot_general(twice, gains[which], NT, preferred_element_type=F32)
        row = list_ref[group, 0, slot]
        total[row] = total[row] + part * (1.0 / (math.pi * POINTS))

    def make(index, which):
        slot = plan_ref[this, index]
        gain = None
        for pair in range(POINTS // 2):
            at = slice(2 * pair * TILE, 2 * (pair + 1) * TILE)
            left = left_ref[slot]
            facing = jnp.dot(left, right[which, 0, :, at], preferred_element_type=F32)
            near = left_ref[slot, :, 0:PLACES]
            toward = jnp.dot(near, right[which, 1, 0:PLACES, at], preferred_element_type=F32)
            spread = jnp.dot(near, right[which, 2, 0:PLACES, at], preferred_element_type=F32)
            over = jnp.maximum(facing, 0.0) * jnp.maximum(toward, 0.0)
            under = spread * spread
            over_a, over_b = over[:, :TILE], over[:, TILE:]
            under_a, under_b = under[:, :TILE], under[:, TILE:]
            term = (over_a * under_b + over_b * under_a) / (under_a * under_b)
            for point in range(POINTS):
                one = term[point * TILE : (point + 1) * TILE]
                gain = one if gain is None else gain + one
        return gain * visible_ref[slot].astype(F32)

    def keep(gain, which):
        high = gain.astype(BF16)
        gains[which, :, 0:TILE] = high
        gains[which, :, TILE:] = (gain - high.astype(F32)).astype(BF16)

    def two_slots(index, carry):
        first = 2 * index
        second = jnp.minimum(first + 1, found - 1)
        live = jnp.where(first + 1 < found, 1.0, 0.0)
        finish(jnp.maximum(first - 2, 0), 0)
        finish(jnp.maximum(first - 1, 0), 1)
        gain_a = make(first, 0)
        gain_b = make(second, 1) * live
        prepare(jnp.minimum(first + 2, found - 1), 0)
        prepare(jnp.minimum(first + 3, found - 1), 1)
        keep(gain_a, 0)
        keep(gain_b, 1)
        return carry

    @pl.when(found > 0)
    def _():
        gains[...] = jnp.zeros_like(gains)
        prepare(0, 0)
        prepare(jnp.minimum(1, found - 1), 1)
        trips = (found + 1) // 2
        lax.fori_loop(0, trips, two_slots, 0)
        finish(2 * trips - 2, 0)
        finish(jnp.minimum(2 * trips - 1, found - 1), 1)


def own_kernel(
    half_tiles, list_ref, plan_ref, static_ref, spot_ref, left_ref, centre_ref,
    visible_ref, rad_ref, points_ref, tiles_hbm, total_ref, tiles, arrived, words, away, right, gains,
):
    copy = pltpu.make_async_copy(tiles_hbm, tiles, arrived)
    copy.start()
    total_ref[...] = jnp.zeros_like(total_ref)
    slots_of_half(
        half_tiles, False, list_ref, plan_ref, spot_ref, left_ref, centre_ref,
        visible_ref, rad_ref, [points_ref], total_ref, words, away, right, gains,
    )
    copy.wait()
    for first in range(0, tiles.shape[0], BATCH):
        parts = []
        for one in range(first, first + BATCH):
            rad = radiosity_of(rad_ref, spot_ref[one])
            parts.append(lax.dot_general(rad, tiles[one], NT, preferred_element_type=F32))
        for step, part in enumerate(parts):
            row = static_ref[0, first + step]
            total_ref[row] = total_ref[row] + part


def other_kernel(
    half_tiles, out_tiles, list_ref, plan_ref, spot_ref, left_ref, centre_ref, visible_ref, rad_ref,
    own_ref, points_ref, sum_ref, keep_ref, send_ref, total, words, away, right, gains,
):
    group = lax.axis_index("cols")
    total[...] = sum_ref[...]
    slots_of_half(
        half_tiles, True, list_ref, plan_ref, spot_ref, left_ref, centre_ref,
        visible_ref, rad_ref, [own_ref, points_ref], total, words, away, right, gains,
    )
    for tile in range(out_tiles):
        at = slice(tile * TILE, (tile + 1) * TILE)
        keep_ref[:, at] = total[group * out_tiles + tile]
        send_ref[:, at] = total[(1 - group) * out_tiles + tile]


def body(
    radiosity,
    emission,
    material,
    reflectance,
    static_tiles,
    static_index,
    row_geometry,
    array_geometry,
    array_owner,
    array_index,
    array_count,
    visibility,
):
    rows = lax.axis_size("rows")
    me = lax.axis_index("rows")
    owner = array_owner[0]
    bands, patches = radiosity.shape
    own_tiles = patches // TILE
    row_tiles = row_geometry.shape[2] // TILE
    array_tiles = array_geometry.shape[-1] // TILE
    half_tiles = array_tiles // 2
    half_rows = 12 * half_tiles + REFS
    rad_rows = 2 * own_tiles
    slots = visibility.shape[2]
    column_tiles = own_tiles * rows

    levels = rows.bit_length() - 1
    orders = hop_orders(rows)

    def hop(value, level):
        pairs = [
            (2 * row + col, 2 * (row ^ orders[col][level]) + col) for row in range(rows) for col in range(2)
        ]
        return lax.ppermute(value, ("rows", "cols"), pairs)

    def better(mine, theirs, level):
        return jnp.where(((owner ^ me) & bit_of(level, rows)) != 0, theirs, mine)

    half_shape = (*array_geometry.shape[2:4], half_tiles * TILE)
    candidates = in_hbm(array_geometry[0, 0])
    hbm = whole(pltpu.HBM)
    small = pltpu.CompilerParams(vmem_limit_bytes=4 << 20)
    send, rad = pl.pallas_call(
        functools.partial(send_kernel, half_tiles),
        out_shape=(VMEM((half_rows + rad_rows, TILE), jnp.int32), VMEM((rad_rows, TILE), jnp.int32)),
        in_specs=[hbm, hbm],
        out_specs=(whole(), whole()),
        scratch_shapes=[
            VMEM(half_shape, F32),
            VMEM(radiosity.shape, radiosity.dtype),
            pltpu.SemaphoreType.DMA((7,)),
        ],
        compiler_params=small,
        name="send",
    )(candidates, in_hbm(radiosity))
    keep, geometry = pl.pallas_call(
        functools.partial(keep_kernel, half_tiles),
        out_shape=(VMEM((half_rows, TILE), jnp.int32), VMEM(row_geometry.shape, F32)),
        in_specs=[hbm, hbm],
        out_specs=(whole(), whole()),
        scratch_shapes=[VMEM(half_shape, F32), pltpu.SemaphoreType.DMA((7,))],
        compiler_params=small,
        name="keep",
    )(candidates, in_hbm(row_geometry))
    smem = whole(pltpu.SMEM)
    lists = array_index[0]
    counts = array_count[0]

    def rows_call(low, high, after, *so_far):
        out_shape = [VMEM((slots, POINTS * TILE, TILE), BF16), VMEM((8, TILE), F32)]
        out_specs = [whole(), whole()]
        if not so_far:
            out_shape.append(jax.ShapeDtypeStruct((3, slots + 1), jnp.int32))
            out_specs.append(smem)
        return pl.pallas_call(
            functools.partial(rows_kernel, low, high, half_tiles),
            out_shape=out_shape,
            in_specs=[smem, smem, whole(), whole(pl.ANY)] + [whole()] * len(so_far),
            out_specs=out_specs,
            input_output_aliases={4: 0, 5: 1} if so_far else {},
            scratch_shapes=[VMEM((POINTS * 64, TILE), F32)],
            compiler_params=small,
            name="rows_high" if so_far else "rows_low",
        )(lists, counts, geometry, after, *so_far)

    for level in range(levels):
        got = hop(send, level)
        if level == 1:
            left, centre, plan = rows_call(0, slots // 2, keep)
            got, left = lax.optimization_barrier((got, left))
        keep = better(keep, got[:half_rows], level)
        rad = jnp.concatenate([rad, got[half_rows:]], axis=0)
        send = jnp.concatenate([keep, rad], axis=0)
        if level == 1:
            left, centre = rows_call(slots // 2, slots, keep, left, centre)
    other = hop(keep, 0)

    def spot(column_tile):
        holder = (column_tile // own_tiles) ^ me
        place = jnp.zeros_like(column_tile)
        for level in range(levels):
            place = place + jnp.where((holder & bit_of(level, rows)) != 0, 1 << level, 0)
        return place * own_tiles + column_tile % own_tiles

    group = lax.axis_index("cols")
    static_list = static_index[0, 0]
    spots = spot(jnp.concatenate([static_list[1], column_tiles - array_tiles + lists[group, 1]]))
    onehot = (jnp.arange(reflectance.shape[1], dtype=jnp.int32)[:, None] == material[None, :]).astype(F32)
    albedo = jnp.dot(reflectance, onehot, precision=lax.Precision.HIGHEST)

    scratch = [
        VMEM((2, half_rows + 16, TILE), jnp.int32),
        VMEM((2, 8, POINTS * TILE), F32),
        VMEM((2, 3, TILE, POINTS * TILE), BF16),
        VMEM((2, TILE, 2 * TILE), BF16),
    ]
    params = pltpu.CompilerParams(vmem_limit_bytes=12 << 20)
    sums = pl.pallas_call(
        functools.partial(own_kernel, half_tiles),
        out_shape=VMEM((row_tiles, bands, TILE), F32),
        in_specs=[smem] * 4 + [whole()] * 5 + [whole(pltpu.HBM)],
        out_specs=whole(),
        scratch_shapes=[
            VMEM(static_tiles.shape[2:], static_tiles.dtype),
            pltpu.SemaphoreType.DMA,
        ]
        + scratch,
        compiler_params=params,
        name="own",
    )(
        lists, plan, static_list, spots, left, centre, visibility[0, 0], rad, keep,
        in_hbm(static_tiles[0, 0]),
    )
    shape = jax.ShapeDtypeStruct((bands, patches), F32)
    mine, sent = pl.pallas_call(
        functools.partial(other_kernel, half_tiles, row_tiles // 2),
        out_shape=(shape, shape),
        in_specs=[smem] * 3 + [whole()] * 7,
        out_specs=(whole(), whole()),
        scratch_shapes=[VMEM((row_tiles, bands, TILE), F32)] + scratch,
        compiler_params=params,
        name="other",
    )(lists, plan, spots, left, centre, visibility[0, 0], rad, keep, other, sums)
    arrived = lax.ppermute(sent, "cols", [(0, 1), (1, 0)])
    return emission + albedo * (mine + arrived)


def solution(mesh):
    in_specs = (
        P(None, ("groups", "rows", "cols")),
        P(None, ("groups", "rows", "cols")),
        P(("groups", "rows", "cols")),
        P(),
        P(("groups", "rows"), "cols", None, None, None),
        P(("groups", "rows"), "cols", None, None),
        P(None, None, ("groups", "rows")),
        P(("groups", "cols"), "rows", None, None, None),
        P(("groups", "cols")),
        P(("groups", "rows"), None, None, None),
        P(("groups", "rows"), None),
        P(("groups", "rows"), "cols", None, None, None),
    )
    out_specs = P(None, ("groups", "rows", "cols"))
    return jax.shard_map(body, mesh=mesh, in_specs=in_specs, out_specs=out_specs, check_vma=False)
```

```python
import functools
import math

import jax
import jax.numpy as jnp
from jax import lax
from jax.experimental import pallas as pl
from jax.experimental.pallas import tpu as pltpu
from jax.sharding import PartitionSpec as P

TILE = 128
POINTS = 4
POS = 2.0**13
MOM = 2.0**19
RAD = 2.0**11
BATCH = 16
PLACES = 64
REFS = 8
GROUP = 16 * 12
F32 = jnp.float32
BF16 = jnp.bfloat16
VMEM = pltpu.VMEM
NT = (((1,), (1,)), ((), ()))


def hop_orders(rows):
    high = [rows >> shift for shift in range(1, rows.bit_length() - 1)]
    return [1] + high, high + [1]


def bit_of(level, rows):
    first, second = hop_orders(rows)
    return jnp.where(lax.axis_index("cols") == 0, first[level], second[level])


def held_half():
    return ((lax.axis_index("rows") & bit_of(0, lax.axis_size("rows"))) != 0).astype(jnp.int32)


def whole(memory_space=VMEM):
    return pl.BlockSpec(memory_space=memory_space)


def in_hbm(value):
    return pltpu.with_memory_space_constraint(value, pltpu.HBM)


def parts3(value):
    first = value.astype(BF16)
    rest = value - first.astype(F32)
    second = rest.astype(BF16)
    third = (rest - second.astype(F32)).astype(BF16)
    return first, second, third


def encode_points(half_tiles, half, geo_hbm, geo_ref, arrived, out_ref):
    lanes = half_tiles * TILE
    part = pl.ds(pl.multiple_of(half * lanes, TILE), lanes)
    fields = [
        pltpu.make_async_copy(geo_hbm.at[field, :, part], geo_ref.at[field], arrived.at[field])
        for field in range(6)
    ]
    for field in (3, 4, 5, 0, 1, 2):
        fields[field].start()
    for field in (3, 4, 5):
        fields[field].wait()
    angles = jnp.concatenate([geo_ref[3], geo_ref[4]], axis=0)
    sines, cosines = jnp.sin(angles), jnp.cos(angles)
    area = geo_ref[5]
    normal = (
        sines[0:4] * cosines[4:8],
        sines[0:4] * sines[4:8],
        cosines[0:4],
    )
    point_rows = 12 * half_tiles
    for axis in range(3):
        fields[axis].wait()
        place = geo_ref[axis]
        centre = jnp.floor(place[0:1, 0:1] + 0.5)
        moved = jnp.floor((place - centre) * POS + 0.5).astype(jnp.int32)
        moved = jnp.clip(moved, -32768, 32767)
        moment = jnp.floor(area * normal[axis] * MOM + 0.5).astype(jnp.int32)
        moment = jnp.clip(moment, -32768, 32767)
        words = (moved << 16) | (moment & 65535)
        for tile in range(half_tiles):
            row = 12 * tile + 4 * axis
            out_ref[row : row + 4, :] = words[:, tile * TILE : (tile + 1) * TILE]
        row = point_rows + axis
        out_ref[row : row + 1, :] = jnp.broadcast_to(centre.astype(jnp.int32), (1, TILE))
    out_ref[point_rows + 3 : point_rows + REFS, :] = jnp.zeros((REFS - 3, TILE), jnp.int32)


def send_kernel(half_tiles, geo_hbm, rad_hbm, send_ref, words_ref, geo_ref, rad_ref, arrived):
    own_rad = pltpu.make_async_copy(rad_hbm, rad_ref, arrived.at[6])
    own_rad.start()
    encode_points(half_tiles, 1 - held_half(), geo_hbm, geo_ref, arrived, send_ref)
    own_rad.wait()
    rad = (rad_ref[...].astype(F32) * RAD).astype(jnp.int32)
    rad = (rad[0:2] << 16) | rad[2:4]
    for tile in range(rad.shape[1] // TILE):
        words_ref[2 * tile : 2 * tile + 2, :] = rad[:, tile * TILE : (tile + 1) * TILE]
    send_ref[12 * half_tiles + REFS :, :] = words_ref[...]


def keep_kernel(half_tiles, geo_hbm, row_hbm, keep_ref, row_ref, geo_ref, arrived):
    rows = pltpu.make_async_copy(row_hbm, row_ref, arrived.at[6])
    rows.start()
    encode_points(half_tiles, held_half(), geo_hbm, geo_ref, arrived, keep_ref)
    rows.wait()


def make_plan(half_tiles, list_ref, count_ref, plan_ref):
    group = lax.axis_index("cols")
    held = held_half()
    dummy = plan_ref.shape[1] - 1

    def pick(slot, seen):
        late = (list_ref[group, 1, slot] // half_tiles) ^ held
        plan_ref[0, jnp.where(late == 0, seen[0], dummy)] = slot
        plan_ref[1, jnp.where(late == 1, seen[1], dummy)] = slot
        return seen[0] + 1 - late, seen[1] + late

    first, found = lax.fori_loop(0, count_ref[group], pick, (jnp.int32(0), jnp.int32(0)))
    spare = first % 2
    plan_ref[1, jnp.where(spare == 1, found, dummy)] = plan_ref[0, jnp.maximum(first - 1, 0)]
    plan_ref[2, 0] = first - spare
    plan_ref[2, 1] = found + spare


def rows_kernel(low, high, half_tiles, list_ref, count_ref, geo_ref, after, *refs):
    if low == 0:
        left_ref, centre_ref, plan_ref, columns = refs
        make_plan(half_tiles, list_ref, count_ref, plan_ref)
    else:
        left_ref, centre_ref, columns = refs[-3:]
    group = lax.axis_index("cols")
    columns[...] = jnp.zeros_like(columns)
    lane_row = lax.broadcasted_iota(jnp.int32, (8, TILE), 0)
    ones = jnp.where(lane_row < 3, 1.0, 0.0).astype(F32)
    blank = jnp.zeros((8, TILE), F32)
    centre_ref[...] = blank
    centre = []
    for axis in range(3):
        first = jnp.floor(geo_ref[axis, 0:1, 0:1] + 0.5)
        centre.append(first)
        centre_ref[axis : axis + 1, :] = jnp.broadcast_to(first, (1, TILE))

    def one_slot(slot, carry):
        start = pl.multiple_of(list_ref[group, 0, slot] * TILE, TILE)
        slab = [geo_ref[field, :, pl.ds(start, TILE)] for field in range(5)]
        place = [slab[axis] - centre[axis] for axis in range(3)]
        angles = jnp.concatenate([slab[3], slab[4]], axis=0)
        sines, cosines = jnp.sin(angles), jnp.cos(angles)
        normal = (sines[0:4] * cosines[4:8], sines[0:4] * sines[4:8], cosines[0:4])
        shift = -(normal[0] * place[0] + normal[1] * place[1] + normal[2] * place[2])
        square = place[0] * place[0] + place[1] * place[1] + place[2] * place[2]

        def put(row, value):
            columns[pl.ds(row, POINTS, stride=64), :] = value.astype(F32)

        for axis in range(3):
            for part, value in enumerate(parts3(normal[axis])):
                put(8 * part + axis, value)
            for part, value in enumerate(parts3(place[axis])):
                put(32 + 8 * part + axis, value)
        for part, value in enumerate(parts3(shift)):
            put(24 + part, value)
        for part, value in enumerate(parts3(square)):
            put(56 + part, value)
        for point in range(POINTS):
            block = [columns[64 * point + 8 * i : 64 * point + 8 * i + 8, :] for i in range(8)]
            n1, n2, n3, c, x1, x2, x3, q = block
            both = [q, x1, x1, x1, x2, x2, x3, ones, n1, n1, n1, n2, n2, n3, c, blank]
            at = pl.ds(point * TILE, TILE)
            left_ref[slot, at, :] = jnp.concatenate(both, axis=0).astype(BF16).T
        return carry

    lax.fori_loop(low, jnp.minimum(count_ref[group], high), one_slot, 0)


def radiosity_of(rad_ref, spot):
    pair = rad_ref[pl.ds(2 * spot, 2), :]
    both = jnp.concatenate([pair >> 16, pair & 65535], axis=0)
    return (both.astype(F32) * (1.0 / RAD)).astype(BF16)


def slots_of_half(
    half_tiles, last_half, list_ref, plan_ref, spot_ref, left_ref, centre_ref, visible_ref, rad_ref,
    points, total, words, away, right, gains,
):
    group = lax.axis_index("cols")
    held = held_half()
    point_rows = 12 * half_tiles
    sub = lax.broadcasted_iota(jnp.int32, (8, POINTS * TILE), 0)
    valid = sub < 3
    for half, points_ref in enumerate(points):
        words[half, 0 : point_rows + REFS, :] = points_ref[...]
        apart = points_ref[point_rows:, :].astype(F32) - centre_ref[...]
        away[half] = jnp.concatenate([apart] * POINTS, axis=1)
    blank = jnp.zeros((8, POINTS * TILE), F32)
    ones = jnp.where(valid, 1.0, 0.0).astype(F32)

    def half_of(slot):
        return (list_ref[group, 1, slot] // half_tiles) ^ held

    this = int(last_half)
    found = plan_ref[2, this]

    def stack3(value):
        first, second, third = (part.astype(F32) for part in parts3(value))
        return jnp.where(sub == 0, first, jnp.where(sub == 1, second, jnp.where(valid, third, 0.0)))

    def split(value):
        return [part.astype(F32) for part in parts3(value)]

    def prepare(index, which):
        slot = plan_ref[this, index]
        half = half_of(slot) if last_half else 0
        start = (list_ref[group, 1, slot] % half_tiles) * 12
        word = jnp.concatenate(
            [words[half, pl.ds(start + point, 8, stride=POINTS), :] for point in range(POINTS)], axis=1
        )
        place = jnp.where(valid, (word >> 16).astype(F32) * (1.0 / POS) + away[half], 0.0)
        moment = jnp.where(valid, ((word << 16) >> 16).astype(F32) * (1.0 / MOM), 0.0)
        area = jnp.sqrt(jnp.sum(moment * moment, axis=0, keepdims=True))
        shift = stack3(-jnp.sum(moment * place, axis=0, keepdims=True))
        square = stack3(jnp.sum(place * place, axis=0, keepdims=True) + area)
        x1, x2, x3 = split(place)
        m1, m2, m3 = split(moment)
        y1, y2, y3 = -2.0 * x1, -2.0 * x2, -2.0 * x3
        right_f = [blank] * 8 + [x1, x2, x3, x1, x2, x1, ones, blank]
        right[which, 0] = jnp.concatenate(right_f, axis=0).astype(BF16)
        right_t = jnp.concatenate([blank, m1, m2, m3, m1, m2, m1, shift], axis=0)
        right[which, 1, 0:PLACES] = right_t.astype(BF16)
        right_s = jnp.concatenate([ones, y1, y2, y3, y1, y2, y1, square], axis=0)
        right[which, 2, 0:PLACES] = right_s.astype(BF16)

    def finish(index, which):
        slot = plan_ref[this, index]
        rad = radiosity_of(rad_ref, spot_ref[spot_ref.shape[0] - list_ref.shape[2] + slot])
        twice = jnp.concatenate([rad, rad], axis=1)
        part = lax.dot_general(twice, gains[which], NT, preferred_element_type=F32)
        row = list_ref[group, 0, slot]
        total[row] = total[row] + part * (1.0 / (math.pi * POINTS))

    def make(index, which):
        slot = plan_ref[this, index]
        gain = None
        for pair in range(POINTS // 2):
            at = slice(2 * pair * TILE, 2 * (pair + 1) * TILE)
            left = left_ref[slot]
            facing = jnp.dot(left, right[which, 0, :, at], preferred_element_type=F32)
            near = left_ref[slot, :, 0:PLACES]
            toward = jnp.dot(near, right[which, 1, 0:PLACES, at], preferred_element_type=F32)
            spread = jnp.dot(near, right[which, 2, 0:PLACES, at], preferred_element_type=F32)
            over = jnp.maximum(facing, 0.0) * jnp.maximum(toward, 0.0)
            under = spread * spread
            over_a, over_b = over[:, :TILE], over[:, TILE:]
            under_a, under_b = under[:, :TILE], under[:, TILE:]
            term = (over_a * under_b + over_b * under_a) / (under_a * under_b)
            for point in range(POINTS):
                one = term[point * TILE : (point + 1) * TILE]
                gain = one if gain is None else gain + one
        return gain * visible_ref[slot].astype(F32)

    def keep(gain, which):
        high = gain.astype(BF16)
        gains[which, :, 0:TILE] = high
        gains[which, :, TILE:] = (gain - high.astype(F32)).astype(BF16)

    def two_slots(index, carry):
        first = 2 * index
        second = jnp.minimum(first + 1, found - 1)
        live = jnp.where(first + 1 < found, 1.0, 0.0)
        finish(jnp.maximum(first - 2, 0), 0)
        finish(jnp.maximum(first - 1, 0), 1)
        gain_a = make(first, 0)
        gain_b = make(second, 1) * live
        prepare(jnp.minimum(first + 2, found - 1), 0)
        prepare(jnp.minimum(first + 3, found - 1), 1)
        keep(gain_a, 0)
        keep(gain_b, 1)
        return carry

    @pl.when(found > 0)
    def _():
        gains[...] = jnp.zeros_like(gains)
        prepare(0, 0)
        prepare(jnp.minimum(1, found - 1), 1)
        trips = (found + 1) // 2
        lax.fori_loop(0, trips // 2, lambda i, c: two_slots(2 * i + 1, two_slots(2 * i, c)), 0)

        @pl.when(trips % 2 == 1)
        def _():
            two_slots(trips - 1, 0)

        finish(2 * trips - 2, 0)
        finish(jnp.minimum(2 * trips - 1, found - 1), 1)


def own_kernel(
    half_tiles, list_ref, plan_ref, static_ref, spot_ref, left_ref, centre_ref,
    visible_ref, rad_ref, points_ref, tiles_hbm, total_ref, tiles, arrived, words, away, right, gains,
):
    copy = pltpu.make_async_copy(tiles_hbm, tiles, arrived)
    copy.start()
    total_ref[...] = jnp.zeros_like(total_ref)
    slots_of_half(
        half_tiles, False, list_ref, plan_ref, spot_ref, left_ref, centre_ref,
        visible_ref, rad_ref, [points_ref], total_ref, words, away, right, gains,
    )
    copy.wait()
    for first in range(0, tiles.shape[0], BATCH):
        parts = []
        for one in range(first, first + BATCH):
            rad = radiosity_of(rad_ref, spot_ref[one])
            parts.append(lax.dot_general(rad, tiles[one], NT, preferred_element_type=F32))
        for step, part in enumerate(parts):
            row = static_ref[0, first + step]
            total_ref[row] = total_ref[row] + part


def other_kernel(
    half_tiles, out_tiles, list_ref, plan_ref, spot_ref, left_ref, centre_ref, visible_ref, rad_ref,
    own_ref, points_ref, sum_ref, keep_ref, send_ref, total, words, away, right, gains,
):
    group = lax.axis_index("cols")
    total[...] = sum_ref[...]
    slots_of_half(
        half_tiles, True, list_ref, plan_ref, spot_ref, left_ref, centre_ref,
        visible_ref, rad_ref, [own_ref, points_ref], total, words, away, right, gains,
    )
    for tile in range(out_tiles):
        at = slice(tile * TILE, (tile + 1) * TILE)
        keep_ref[:, at] = total[group * out_tiles + tile]
        send_ref[:, at] = total[(1 - group) * out_tiles + tile]


def body(
    radiosity,
    emission,
    material,
    reflectance,
    static_tiles,
    static_index,
    row_geometry,
    array_geometry,
    array_owner,
    array_index,
    array_count,
    visibility,
):
    rows = lax.axis_size("rows")
    me = lax.axis_index("rows")
    owner = array_owner[0]
    bands, patches = radiosity.shape
    own_tiles = patches // TILE
    row_tiles = row_geometry.shape[2] // TILE
    array_tiles = array_geometry.shape[-1] // TILE
    half_tiles = array_tiles // 2
    half_rows = 12 * half_tiles + REFS
    rad_rows = 2 * own_tiles
    slots = visibility.shape[2]
    column_tiles = own_tiles * rows

    levels = rows.bit_length() - 1
    orders = hop_orders(rows)

    def hop(value, level):
        pairs = [
            (2 * row + col, 2 * (row ^ orders[col][level]) + col) for row in range(rows) for col in range(2)
        ]
        return lax.ppermute(value, ("rows", "cols"), pairs)

    def better(mine, theirs, level):
        return jnp.where(((owner ^ me) & bit_of(level, rows)) != 0, theirs, mine)

    half_shape = (*array_geometry.shape[2:4], half_tiles * TILE)
    candidates = in_hbm(array_geometry[0, 0])
    hbm = whole(pltpu.HBM)
    small = pltpu.CompilerParams(vmem_limit_bytes=4 << 20)
    send, rad = pl.pallas_call(
        functools.partial(send_kernel, half_tiles),
        out_shape=(VMEM((half_rows + rad_rows, TILE), jnp.int32), VMEM((rad_rows, TILE), jnp.int32)),
        in_specs=[hbm, hbm],
        out_specs=(whole(), whole()),
        scratch_shapes=[
            VMEM(half_shape, F32),
            VMEM(radiosity.shape, radiosity.dtype),
            pltpu.SemaphoreType.DMA((7,)),
        ],
        compiler_params=small,
        name="send",
    )(candidates, in_hbm(radiosity))
    keep, geometry = pl.pallas_call(
        functools.partial(keep_kernel, half_tiles),
        out_shape=(VMEM((half_rows, TILE), jnp.int32), VMEM(row_geometry.shape, F32)),
        in_specs=[hbm, hbm],
        out_specs=(whole(), whole()),
        scratch_shapes=[VMEM(half_shape, F32), pltpu.SemaphoreType.DMA((7,))],
        compiler_params=small,
        name="keep",
    )(candidates, in_hbm(row_geometry))
    smem = whole(pltpu.SMEM)
    lists = array_index[0]
    counts = array_count[0]

    def rows_call(low, high, after, *so_far):
        out_shape = [VMEM((slots, POINTS * TILE, TILE), BF16), VMEM((8, TILE), F32)]
        out_specs = [whole(), whole()]
        if not so_far:
            out_shape.append(jax.ShapeDtypeStruct((3, slots + 1), jnp.int32))
            out_specs.append(smem)
        return pl.pallas_call(
            functools.partial(rows_kernel, low, high, half_tiles),
            out_shape=out_shape,
            in_specs=[smem, smem, whole(), whole(pl.ANY)] + [whole()] * len(so_far),
            out_specs=out_specs,
            input_output_aliases={4: 0, 5: 1} if so_far else {},
            scratch_shapes=[VMEM((POINTS * 64, TILE), F32)],
            compiler_params=small,
            name="rows_high" if so_far else "rows_low",
        )(lists, counts, geometry, after, *so_far)

    for level in range(levels):
        got = hop(send, level)
        if level == 1:
            left, centre, plan = rows_call(0, slots // 2, keep)
            got, left = lax.optimization_barrier((got, left))
        keep = better(keep, got[:half_rows], level)
        rad = jnp.concatenate([rad, got[half_rows:]], axis=0)
        send = jnp.concatenate([keep, rad], axis=0)
        if level == 1:
            left, centre = rows_call(slots // 2, slots, keep, left, centre)
    other = hop(keep, 0)

    def spot(column_tile):
        holder = (column_tile // own_tiles) ^ me
        place = jnp.zeros_like(column_tile)
        for level in range(levels):
            place = place + jnp.where((holder & bit_of(level, rows)) != 0, 1 << level, 0)
        return place * own_tiles + column_tile % own_tiles

    group = lax.axis_index("cols")
    static_list = static_index[0, 0]
    spots = spot(jnp.concatenate([static_list[1], column_tiles - array_tiles + lists[group, 1]]))
    onehot = (jnp.arange(reflectance.shape[1], dtype=jnp.int32)[:, None] == material[None, :]).astype(F32)
    albedo = jnp.dot(reflectance, onehot, precision=lax.Precision.HIGHEST)

    scratch = [
        VMEM((2, half_rows + 16, TILE), jnp.int32),
        VMEM((2, 8, POINTS * TILE), F32),
        VMEM((2, 3, TILE, POINTS * TILE), BF16),
        VMEM((2, TILE, 2 * TILE), BF16),
    ]
    params = pltpu.CompilerParams(vmem_limit_bytes=12 << 20)
    sums = pl.pallas_call(
        functools.partial(own_kernel, half_tiles),
        out_shape=VMEM((row_tiles, bands, TILE), F32),
        in_specs=[smem] * 4 + [whole()] * 5 + [whole(pltpu.HBM)],
        out_specs=whole(),
        scratch_shapes=[
            VMEM(static_tiles.shape[2:], static_tiles.dtype),
            pltpu.SemaphoreType.DMA,
        ]
        + scratch,
        compiler_params=params,
        name="own",
    )(
        lists, plan, static_list, spots, left, centre, visibility[0, 0], rad, keep,
        in_hbm(static_tiles[0, 0]),
    )
    shape = jax.ShapeDtypeStruct((bands, patches), F32)
    mine, sent = pl.pallas_call(
        functools.partial(other_kernel, half_tiles, row_tiles // 2),
        out_shape=(shape, shape),
        in_specs=[smem] * 3 + [whole()] * 7,
        out_specs=(whole(), whole()),
        scratch_shapes=[VMEM((row_tiles, bands, TILE), F32)] + scratch,
        compiler_params=params,
        name="other",
    )(lists, plan, spots, left, centre, visibility[0, 0], rad, keep, other, sums)
    arrived = lax.ppermute(sent, "cols", [(0, 1), (1, 0)])
    return emission + albedo * (mine + arrived)


def solution(mesh):
    in_specs = (
        P(None, ("groups", "rows", "cols")),
        P(None, ("groups", "rows", "cols")),
        P(("groups", "rows", "cols")),
        P(),
        P(("groups", "rows"), "cols", None, None, None),
        P(("groups", "rows"), "cols", None, None),
        P(None, None, ("groups", "rows")),
        P(("groups", "cols"), "rows", None, None, None),
        P(("groups", "cols")),
        P(("groups", "rows"), None, None, None),
        P(("groups", "rows"), None),
        P(("groups", "rows"), "cols", None, None, None),
    )
    out_specs = P(None, ("groups", "rows", "cols"))
    return jax.shard_map(body, mesh=mesh, in_specs=in_specs, out_specs=out_specs, check_vma=False)
```
